32 devices in a mesh: lon: 8 (over z, core), lat: 4 (over y, x).
Axes of the slice: x: 2, y: 2, z: 4, core: 2. Of those that a mesh axis runs over, the one named last changes fastest.
Arguments:
- tracers: float32 [32, 32, 16384], P(None, 'lat', 'lon'), may hold values from 0.1 to 10
- courant: float32 [2, 32, 256], P(None, 'lat', 'lon'), may hold values from -0.45 to 0.45
- switches: int32 [2, 32, 256], P(None, 'lat', 'lon'), may hold values 0 or 1
- day_flags: int32 [32, 256], P('lat', 'lon'), may hold values from 0 to 1, as said below
- diffusion_counts: int32 [32, 256], P('lat', 'lon'), may hold values from 1 to 8
- night_rates: float32 [32, 32], replicated, may hold values from -0.18 to 0.18
- photo_rates: float32 [32, 32], replicated, may hold values from -0.24 to 0.24
- level_light: float32 [64], replicated, may hold values from 0.1 to 1
- self_loss: float32 [32], replicated, may hold values from 0.001 to 0.05
- vertical_mixing: float32 [63], replicated, may hold values from 0.05 to 0.45
Outputs:
- tracers_out: float32 [32, 32, 16384], P(None, 'lat', 'lon')
The draws below stay inside these ranges and needn't reach their ends.
Inputs may be any that keep to these rules, and one draw needn't show every extreme that they name: `day_flags`: in every latitude row exactly half of the 256 columns are day columns, forming one contiguous band around the longitude cycle.
All inputs are finite; a program needn't handle non-finite values. No bound on the sum of `switches` on one device may be relied on, other than what follows from the above.
Results may differ from the reference program's by a relative error of at most 0.0003.
Values sent between devices are 32-bit elements; how exact they have to be, the bound alone decides.
A program may use at most 64 MiB of HBM per device.

```python
import math
import jax
import jax.numpy as jnp
from jax import lax

SPECIES = 32
LEVELS = 64
CHEM = 6
KMAX = 8
NLAT = 32
NLON = 256


def column_plan(key):
    base_key = jax.random.fold_in(key, 4099)
    key_offset, key_jitter, key_night, key_day = jax.random.split(base_key, 4)
    offset = jax.random.randint(key_offset, (), 0, NLON)
    jitter = jax.random.randint(key_jitter, (NLAT, 1), -2, 3)
    longitude = jnp.arange(NLON, dtype=jnp.int32)[None, :]
    daylight = ((longitude - offset - jitter) % NLON < NLON // 2).astype(jnp.int32)
    night_counts = jax.random.randint(key_night, (NLAT, NLON), 1, KMAX // 2 + 1)
    day_counts = jax.random.randint(key_day, (NLAT, NLON), KMAX // 2, KMAX + 1)
    substeps = jnp.where(daylight == 1, day_counts, night_counts).astype(jnp.int32)
    substeps = substeps.at[0, 0].set(KMAX).at[NLAT - 1, NLON - 1].set(1)
    return (daylight, substeps)


def draw_day_flags(key, part):
    return column_plan(key)[0]


def draw_diffusion_counts(key, part):
    return column_plan(key)[1]


def set_ends(values, stream_key, low, top_value):
    index_at = [jax.random.randint(jax.random.fold_in(stream_key, axis), (), 0, length) for axis, length in enumerate(values.shape)]
    main_axis = values.shape.index(max(values.shape))
    next_to = index_at[:main_axis] + [(index_at[main_axis] + 1) % values.shape[main_axis]] + index_at[main_axis + 1:]
    return values.at[tuple(index_at)].set(low).at[tuple(next_to)].set(top_value)


def block_scale(rng, dims, cuts, smallest, top_value):
    def one(position, blocks):
        heights = jax.random.uniform(jax.random.fold_in(jax.random.fold_in(rng, 6), position), (blocks,), jnp.float32, smallest / len(cuts), top_value / len(cuts))
        return jnp.repeat(jnp.exp(heights), dims[position] // blocks).reshape((-1,) + (1,) * (len(dims) - position - 1))

    factor_of = one(*cuts[0])
    for cut in cuts[1:]:
        factor_of = factor_of * one(*cut)
    return factor_of


def bell_draw(key, shape, spread, most, held_as=jnp.bfloat16):
    entries = jax.random.normal(key, shape, jnp.float32) * spread
    return jnp.minimum(jnp.maximum(entries, -most), most).astype(held_as)


def setup_inputs(seed: int = 0) -> dict:
    streams_of = jax.random.split(jax.random.key(seed), 11)
    return {
        "tracers": jnp.clip(jnp.exp(math.log(10.0) - 4.6051702 * jax.random.uniform(streams_of[0], (SPECIES, NLAT, NLON * LEVELS), jnp.float32) ** block_scale(streams_of[0], (SPECIES, NLAT, NLON * LEVELS), ((1, 4), (2, 8)), -0.2, 0.2)), 0.1, 10.0),
        "courant": jnp.clip(jax.random.uniform(streams_of[1], (2, NLAT, NLON), jnp.float32, -0.45, 0.45) * block_scale(streams_of[1], (2, NLAT, NLON), ((1, 4), (2, 8)), -0.4, 0.0), -0.45, 0.45),
        "switches": set_ends((jax.random.randint(streams_of[2], (2, NLAT, NLON), 0, 4) < 3).astype(jnp.int32), jax.random.fold_in(streams_of[2], 1), 0, 1),
        "day_flags": draw_day_flags(jax.random.fold_in(streams_of[10], 71), 0),
        "diffusion_counts": draw_diffusion_counts(jax.random.fold_in(streams_of[10], 71), 0),
        "night_rates": bell_draw(streams_of[5], (SPECIES, SPECIES), 0.03, 0.18, jnp.float32),
        "photo_rates": bell_draw(streams_of[6], (SPECIES, SPECIES), 0.04, 0.24, jnp.float32),
        "level_light": jnp.clip(jnp.exp(jax.random.uniform(streams_of[7], (LEVELS,), jnp.float32, math.log(0.1), math.log(1.0))), 0.1, 1.0),
        "self_loss": jnp.clip(jnp.exp(jax.random.uniform(streams_of[8], (SPECIES,), jnp.float32, math.log(0.001), math.log(0.05))), 0.001, 0.05),
        "vertical_mixing": jnp.clip(jax.random.uniform(streams_of[9], (LEVELS - 1,), jnp.float32, 0.05, 0.45), 0.05, 0.45),
    }


def minmod(left, right):
    return 0.5 * (jnp.sign(left) + jnp.sign(right)) * jnp.minimum(jnp.abs(left), jnp.abs(right))


def advect_sweep(extended, cour, switch, along_axis, cell_count, cell_unit):
    def take_cells(first_cell, number):
        return lax.slice_in_dim(extended, first_cell * cell_unit, (first_cell + number) * cell_unit, axis=along_axis)

    second_left = take_cells(0, cell_count + 1)
    first_left = take_cells(1, cell_count + 1)
    first_right = take_cells(2, cell_count + 1)
    second_right = take_cells(3, cell_count + 1)
    plus_flux = cour * (first_left + 0.5 * (1.0 - cour) * switch * minmod(first_left - second_left, first_right - first_left))
    minus_flux = cour * (first_right - 0.5 * (1.0 + cour) * switch * minmod(first_right - first_left, second_right - first_right))
    face_flux = jnp.where(cour >= 0.0, plus_flux, minus_flux)
    upper_faces = lax.slice_in_dim(face_flux, cell_unit, (cell_count + 1) * cell_unit, axis=along_axis)
    lower_faces = lax.slice_in_dim(face_flux, 0, cell_count * cell_unit, axis=along_axis)
    return take_cells(2, cell_count) - (upper_faces - lower_faces)


def react_mix(tracer_block, daylight, substeps, rate_rows, level_light, self_loss, vertical_mixing, loop_count):
    species = tracer_block.shape[0]
    levels = level_light.shape[0]
    column = daylight.shape[-1]
    sunlight = jnp.repeat(daylight.astype(jnp.float32), levels, axis=-1) * jnp.tile(level_light, column)
    self_term = self_loss.reshape((species,) + (1,) * (tracer_block.ndim - 1))
    for _ in range(CHEM):
        flat = tracer_block.reshape(species, -1)
        joined = jnp.dot(rate_rows, flat, precision=lax.Precision.HIGHEST).reshape((2,) + tracer_block.shape)
        tracer_block = (tracer_block + joined[0] + sunlight * joined[1]) / (1.0 + self_term * tracer_block * tracer_block)
    mixing_faces = jnp.tile(jnp.concatenate([vertical_mixing, jnp.zeros((1,), vertical_mixing.dtype)]), column)
    step_limits = jnp.repeat(substeps, levels, axis=-1)

    def mix_step(step_index, tracer_field):
        edge = jnp.zeros_like(tracer_field[..., :1])
        above_cells = jnp.concatenate([tracer_field[..., 1:], edge], -1)
        level_flux = mixing_faces * (above_cells - tracer_field)
        below_flux = jnp.concatenate([edge, level_flux[..., :-1]], -1)
        return jnp.where(step_index < step_limits, tracer_field + level_flux - below_flux, tracer_field)

    return lax.fori_loop(0, loop_count, mix_step, tracer_block)


def reference(tracers, courant, switches, day_flags, diffusion_counts, night_rates, photo_rates, level_light, self_loss, vertical_mixing):
    switch_float = switches.astype(jnp.float32)
    lon_cour = jnp.concatenate([courant[0], courant[0][:, :1]], 1)
    lon_switch = jnp.concatenate([switch_float[0], switch_float[0][:, :1]], 1)
    row_valid = (jnp.arange(NLAT) >= 1).astype(jnp.float32)[:, None]
    lat_cour = jnp.concatenate([courant[1] * row_valid, jnp.zeros((1, NLON), jnp.float32)], 0)
    lat_switch = jnp.concatenate([switch_float[1], jnp.zeros((1, NLON), jnp.float32)], 0)
    lon_cour = jnp.repeat(lon_cour, LEVELS, axis=1)
    lon_switch = jnp.repeat(lon_switch, LEVELS, axis=1)
    lat_cour = jnp.repeat(lat_cour, LEVELS, axis=1)
    lat_switch = jnp.repeat(lat_switch, LEVELS, axis=1)

    def transport(tracer_field):
        extended = jnp.concatenate([tracer_field[:, -2 * LEVELS:], tracer_field, tracer_field[:, :2 * LEVELS]], 1)
        midway = advect_sweep(extended, lon_cour, lon_switch, 1, NLON, LEVELS)
        extended = jnp.pad(midway, ((2, 2), (0, 0)))
        return advect_sweep(extended, lat_cour, lat_switch, 0, NLAT, 1)

    rate_rows = jnp.concatenate([night_rates, photo_rates], 0)
    advected = lax.map(transport, tracers)

    def column_work(item):
        tracer_block, daylight, substeps = item
        return react_mix(tracer_block, daylight, substeps, rate_rows, level_light, self_loss, vertical_mixing, KMAX)

    reacted = lax.map(column_work, (jnp.moveaxis(advected, 1, 0), day_flags, diffusion_counts))
    return lax.map(transport, jnp.moveaxis(reacted, 0, 1))
```

```python
import functools

import jax
import jax.numpy as jnp
from jax import lax
from jax.experimental import pallas as pl
from jax.experimental.pallas import tpu as pltpu
from jax.sharding import PartitionSpec as P

CHEM = 6
KMAX = 8
EDGE = 2
RUN = 2
AHEAD = 4
MESH = pl.DeviceIdType.MESH


def minmod(x, y):
    return jnp.maximum(jnp.minimum(x, y), 0.0) + jnp.minimum(jnp.maximum(x, y), 0.0)


def face_flux(c, coef, aa, a, b, bb):
    pos = c >= 0.0
    x = jnp.where(pos, a - aa, bb - b)
    return c * (jnp.where(pos, a, b) + coef * minmod(x, b - a))


def build_powers(unit, mix_ref, power_ref):
    source = lax.broadcasted_iota(jnp.int32, (unit, unit), 0)
    target = lax.broadcasted_iota(jnp.int32, (unit, unit), 1)
    up = jnp.broadcast_to(mix_ref[...], (unit, unit))
    down = pltpu.roll(up, 1, 1)
    one = jnp.where(source == target, 1.0 - up - down, 0.0)
    one = jnp.where(source == target + 1, up, one)
    one = jnp.where(source == target - 1, down, one)
    powers = {1: one}
    for n in range(2, KMAX + 1):
        half = n // 2
        powers[n] = jnp.dot(
            powers[half],
            powers[n - half],
            precision=lax.Precision.HIGHEST,
            preferred_element_type=jnp.float32,
        )
    for n, power in powers.items():
        at = slice((n - 1) * unit, n * unit)
        top = power.astype(jnp.bfloat16)
        power_ref[:unit, at] = top
        power_ref[unit : 2 * unit, at] = top
        power_ref[2 * unit :, at] = (power - top.astype(jnp.float32)).astype(jnp.bfloat16)


def kernel(
    unit,
    x_ref,
    courant_ref,
    switch_ref,
    day_ref,
    raw_cnt_ref,
    night_ref,
    photo_ref,
    light_ref,
    raw_loss_ref,
    vertical_ref,
    out_ref,
    comp_ref,
    lonc_ref,
    lonk_ref,
    latc_ref,
    latk_ref,
    sun_ref,
    cnt_ref,
    mix_ref,
    w_ref,
    loss_ref,
    mid_ref,
    mid_halo,
    state_ref,
    again_ref,
    side_raw,
    corner_raw,
    side_ref,
    halo_ref,
    relay_ref,
    power_ref,
    comp_send,
    comp_recv,
    side_send,
    side_recv,
    corner_send,
    corner_recv,
    halo_send,
    halo_recv,
    relay_recv,
    relay_send,
):
    rows, species, lanes = x_ref.shape
    cols = courant_ref.shape[2]
    tiles = lanes // unit
    runs = tiles // RUN
    nlon, nlat = lax.axis_size("lon"), lax.axis_size("lat")
    lon, lat = lax.axis_index("lon"), lax.axis_index("lat")
    east, west = lax.rem(lon + 1, nlon), lax.rem(lon + nlon - 1, nlon)
    has_south, has_north = lat > 0, lat < nlat - 1
    has = (has_south, has_north)
    half = nlat // 2
    relayed = nlat > 2 and nlat % 2 == 0
    is_low_mid, is_high_mid = lat == half - 1, lat == half
    is_mid = jnp.logical_or(is_low_mid, is_high_mid)
    is_relay = jnp.logical_or(lat == 0, lat == nlat - 1)
    relay_of = jnp.where(is_low_mid, nlat - 1, 0)
    relay_to = jnp.where(lat == 0, half - 1, half)
    relay_side = jnp.where(lat == 0, 1, 0)

    spans = []
    for i in range(runs // 2):
        spans += [i * RUN, tiles - (i + 1) * RUN]
    groups = runs // 2
    reach = [(k + 1) * RUN - 1 for k in range(groups)]
    reach[-1] = tiles // 2
    after = [max(r - 1, 0) for r in reach]
    after[-1] = tiles // 2

    def ranges(ends, k):
        first = ends[k - 1] if k else 0
        last = ends[k]
        if last == first:
            return []
        if last == tiles // 2:
            return [(first, tiles - first)]
        return [(first, last), (tiles - last, tiles - first)]

    def lanes_of(first, last):
        return pl.ds(first * unit, (last - first) * unit)

    def run_lanes(i):
        return lanes_of(spans[i], spans[i] + RUN)

    barrier = pltpu.get_barrier_semaphore()

    def greet(to):
        pl.semaphore_signal(barrier, inc=1, device_id=to, device_id_type=MESH)

    for side in (east, west):
        greet({"lon": side})

    @pl.when(has_south)
    def _():
        for side in (lon, east, west):
            greet({"lat": lat - 1, "lon": side})

    @pl.when(has_north)
    def _():
        for side in (lon, east, west):
            greet({"lat": lat + 1, "lon": side})

    if relayed:

        @pl.when(is_mid)
        def _():
            greet({"lat": relay_of})

        @pl.when(is_relay)
        def _():
            greet({"lat": jnp.where(lat == 0, half, half - 1)})

    c_own = courant_ref[...]
    m_own = switch_ref[...].astype(jnp.float32)
    row_own = lax.broadcasted_iota(jnp.int32, c_own[1].shape, 0)
    c_lat = jnp.where(jnp.logical_and(row_own == 0, lat == 0), 0.0, c_own[1])
    comp_ref[0] = jnp.concatenate(
        [c_own[0], slopes(c_own[0], m_own[0]), c_lat, slopes(c_lat, m_own[1])], 1
    )

    for d in range(2):

        @pl.when(jnp.logical_not(has[d]))
        def _():
            for p in range(2):
                halo_ref[p, d] = jnp.zeros(halo_ref.shape[2:], jnp.float32)
            for s in range(2):
                corner_raw[s, d] = jnp.zeros(corner_raw.shape[2:], jnp.float32)
            near = jnp.zeros(comp_ref.shape[1:], jnp.float32)
            comp_ref[2 + d] = near
            comp_ref[4 + d] = near

    peers = 2 + jnp.where(has_south, 3, 0) + jnp.where(has_north, 3, 0)
    if relayed:
        peers = peers + jnp.where(jnp.logical_or(is_mid, is_relay), 1, 0)
    pl.semaphore_wait(barrier, peers)

    def remote(src, dst, send, recv, to):
        return pltpu.make_async_remote_copy(
            src_ref=src,
            dst_ref=dst,
            send_sem=send,
            recv_sem=recv,
            device_id=to,
            device_id_type=MESH,
        )

    def comp_copy(slot, to):
        return remote(
            comp_ref.at[0], comp_ref.at[slot], comp_send.at[slot], comp_recv.at[slot], to
        )

    comp_west = comp_copy(1, {"lon": west})
    comp_up = (comp_copy(2, {"lat": lat + 1}), comp_copy(4, {"lat": lat + 1, "lon": west}))
    comp_down = (comp_copy(3, {"lat": lat - 1}), comp_copy(5, {"lat": lat - 1, "lon": west}))

    def side_raw_copies():
        pairs = ((tiles - 1, 0, east), (0, 1, west))
        return [
            remote(
                x_ref.at[:, :, lanes_of(tile, tile + 1)],
                side_raw.at[s],
                side_send.at[0, 0, s],
                side_recv.at[0, 0, s],
                {"lon": to},
            )
            for tile, s, to in pairs
        ]

    side_rows = ((0, EDGE), (rows - EDGE, EDGE), (EDGE, rows - 2 * EDGE))

    def side_copies(part):
        first, number = side_rows[part]
        held = pl.ds(first, number)
        pairs = ((tiles - 1, 0, east), (0, 1, west))
        return [
            remote(
                state_ref.at[held, :, lanes_of(tile, tile + 1)],
                side_ref.at[s, held],
                side_send.at[1, part, s],
                side_recv.at[1, part, s],
                {"lon": to},
            )
            for tile, s, to in pairs
        ]

    def corner_copies(d):
        pairs = ((tiles - 1, 0, east), (0, 1, west))
        return [
            remote(
                halo_ref.at[0, d, :, :, lanes_of(tile, tile + 1)],
                corner_raw.at[s, d],
                corner_send.at[d, s],
                corner_recv.at[d, s],
                {"lon": to},
            )
            for tile, s, to in pairs
        ]

    def row_of(phase, row, i):
        if phase == 0:
            return x_ref.at[row, :, run_lanes(i)]
        return again_ref.at[row, :, run_lanes(i)]

    def halo_copy(phase, d, i, r):
        row = r if d else rows - EDGE + r
        return remote(
            row_of(phase, row, i),
            halo_ref.at[phase, d, r, :, run_lanes(i)],
            halo_send.at[phase, d, i, r],
            halo_recv.at[phase, d, i, r],
            {"lat": lat - 1 if d else lat + 1},
        )

    def relay_copy(phase, d, i):
        row = 1 if d else rows - 1
        return remote(
            row_of(phase, row, i),
            relay_ref.at[phase, :, run_lanes(i)],
            halo_send.at[phase, d, i, 1],
            relay_recv.at[phase, i],
            {"lat": relay_of},
        )

    def forward_copy(phase, i):
        return remote(
            relay_ref.at[phase, :, run_lanes(i)],
            halo_ref.at[phase, relay_side, 1, :, run_lanes(i)],
            relay_send.at[phase, i],
            halo_recv.at[phase, relay_side, i, 1],
            {"lat": relay_to},
        )

    def halo_start(phase, i):
        if relayed:

            @pl.when(is_low_mid)
            def _():
                relay_copy(phase, 0, i).start()

            @pl.when(is_high_mid)
            def _():
                relay_copy(phase, 1, i).start()

        for d in (1, 0):
            there = has_south if d else has_north
            direct = there
            if relayed:
                direct = jnp.logical_and(there, jnp.logical_not(is_high_mid if d else is_low_mid))

            @pl.when(there)
            def _():
                halo_copy(phase, d, i, 0).start()

            @pl.when(direct)
            def _():
                halo_copy(phase, d, i, 1).start()

    def halo_sent(phase):
        for i in range(runs):
            for d in range(2):

                @pl.when(has_south if d else has_north)
                def _():
                    for r in range(EDGE):
                        halo_copy(phase, d, i, r).wait_send()

            if relayed:

                @pl.when(is_relay)
                def _():
                    forward_copy(phase, i).wait_send()

    def halo_arrive(phase, i):
        for d in range(2):

            @pl.when(has[d])
            def _():
                for r in range(EDGE):
                    halo_copy(phase, d, i, r).wait_recv()

    def forward(phase, i):
        if relayed:
            relay_copy(phase, 0, i).wait_recv()
            forward_copy(phase, i).start()

    def forwards(phase, some):
        if relayed:

            @pl.when(is_relay)
            def _():
                for i in some:
                    forward(phase, i)

    comp_west.start()

    @pl.when(has_north)
    def _():
        for copy in comp_up:
            copy.start()

    @pl.when(has_south)
    def _():
        for copy in comp_down:
            copy.start()

    raw_sides = side_raw_copies()
    for copy in raw_sides:
        copy.start()
    for i in range(min(AHEAD, runs)):
        halo_start(0, i)
    if relayed:

        @pl.when(jnp.logical_not(is_relay))
        def _():
            for i in range(AHEAD, runs):
                halo_start(0, i)

    else:
        for i in range(AHEAD, runs):
            halo_start(0, i)

    def first_forwards(some):
        if relayed:

            @pl.when(is_relay)
            def _():
                for i in some:
                    forward(0, i)
                    if i + AHEAD < runs:
                        halo_start(0, i + AHEAD)

    def spread(plane, target, scale=None):
        left = lax.broadcasted_iota(jnp.int32, (plane.shape[0], unit), 1) < unit // 2
        for j in range(tiles):
            a = jnp.broadcast_to(plane[:, 2 * j : 2 * j + 1], left.shape)
            b = jnp.broadcast_to(plane[:, 2 * j + 1 : 2 * j + 2], left.shape)
            v = jnp.where(left, a, b)
            if scale is not None:
                v = v * scale
            for r in range(plane.shape[0]):
                target(r, slice(j * unit, (j + 1) * unit), v[r : r + 1])

    def into(ref, offset=0):
        def put(r, at, v):
            ref[r + offset, :, at] = v

        return put

    def lon_planes(own, outer, offset):
        for n, ref in enumerate((lonc_ref, lonk_ref)):
            spread(own[:, n * cols : (n + 1) * cols], into(ref, offset))
            last = jnp.broadcast_to(outer[:, n * cols : n * cols + 1], (own.shape[0], unit))
            for r in range(own.shape[0]):
                ref[r + offset, :, lanes:] = last[r : r + 1]

    def prepare_columns():
        mix = vertical_ref[...]
        gap = jnp.zeros((1, 1), jnp.float32)
        mix_ref[...] = jnp.concatenate([mix, gap, mix, gap], 1)
        light = jnp.concatenate([light_ref[...], light_ref[...]], 1)
        spread(day_ref[...].astype(jnp.float32), into(sun_ref), light)
        spread(raw_cnt_ref[...], into(cnt_ref))

    def prepare_rates():
        rates = jnp.concatenate([night_ref[...], photo_ref[...]], 0)
        top = rates.astype(jnp.bfloat16).astype(jnp.float32)
        w_ref[...] = jnp.concatenate([top, top, rates - top], 1).astype(jnp.bfloat16)
        shape = (species, species)
        same = lax.broadcasted_iota(jnp.int32, shape, 0) == lax.broadcasted_iota(jnp.int32, shape, 1)
        spread_loss = jnp.broadcast_to(raw_loss_ref[...], shape)
        loss_ref[...] = jnp.sum(jnp.where(same, spread_loss, 0.0), axis=1, keepdims=True)

    low = lax.broadcasted_iota(jnp.int32, (species, unit), 1) < unit // 2

    def swap(v):
        return pltpu.roll(v, unit // 2, 1)

    def lon_range(tile, store, e, first, last):
        before, here = tile(first - 1), tile(first)
        swapped = swap(here)
        behind = jnp.where(low, swap(before), swapped)
        flux, turned, cell = None, None, None
        for j in range(first, last + 1):
            if j < last:
                later = tile(j + 1)
                later_swapped = swap(later)
                ahead = jnp.where(low, swapped, later_swapped)
            else:
                later, later_swapped, ahead = here, swapped, swapped
            at = slice(j * unit, (j + 1) * unit)
            now = face_flux(lonc_ref[e, :, at], lonk_ref[e, :, at], before, behind, here, ahead)
            now_turned = swap(now)
            if j > first:
                upper = jnp.where(low, turned, now_turned)
                store(slice((j - 1) * unit, j * unit), cell - (upper - flux))
            flux, turned, cell = now, now_turned, here
            before, here, behind, swapped = here, later, ahead, later_swapped

    def lon_sweep(number, view, parts):
        def one(i, carry):
            tile, store, e = view(i)
            for first, last in parts:
                lon_range(tile, store, e, first, last)
            return carry

        lax.fori_loop(0, number, one, 0)

    whole = [(0, tiles)]

    def picker(inside, left, right):
        def tile(j):
            if j < 0:
                return left()
            if j == tiles:
                return right()
            return inside(j, slice(j * unit, (j + 1) * unit))

        return tile

    def raw_view(i):
        tile = picker(
            lambda j, at: x_ref[i, :, at],
            lambda: side_raw[0, i],
            lambda: side_raw[1, i],
        )

        def store(at, v):
            mid_ref[i, :, at] = v

        return tile, store, i + EDGE

    def raw_halo_view(i):
        d, r = i // EDGE, i % EDGE
        tile = picker(
            lambda j, at: halo_ref[0, d, r, :, at],
            lambda: corner_raw[0, d, r],
            lambda: corner_raw[1, d, r],
        )

        def store(at, v):
            mid_halo[d, r, :, at] = v

        return tile, store, r + d * (rows + EDGE)

    def state_view(offset):
        def view(i):
            row = i + offset if offset else i + (i // EDGE) * (rows - 2 * EDGE)
            tile = picker(
                lambda j, at: state_ref[row, :, at],
                lambda: side_ref[0, row],
                lambda: side_ref[1, row],
            )

            def store(at, v):
                again_ref[row, :, at] = v

            return tile, store, row + EDGE

        return view

    def lat_sweep(source, halo, store, spans, parts):
        def sweep(j):
            at = pl.ds(pl.multiple_of(j * unit, unit), unit)

            def cell(row):
                if row < 0:
                    return halo(0, row + EDGE, at)
                if row >= rows:
                    return halo(1, row - rows, at)
                return source[row, :, at]

            for first, last in spans:
                aa, a, b = cell(first - 2), cell(first - 1), cell(first)
                flux = None
                for row in range(first, last + 1):
                    bb = cell(row + 1)
                    now = face_flux(latc_ref[row, :, at], latk_ref[row, :, at], aa, a, b, bb)
                    if flux is not None:
                        store(row - 1, j, a - (now - flux))
                    flux = now
                    aa, a, b = a, b, bb

        count = sum(last - first for first, last in parts)
        each = count // len(parts)

        def one(t, carry):
            j = t + parts[0][0]
            if len(parts) > 1:
                j = j + (t // each) * (parts[1][0] - parts[0][0] - each)
            sweep(j)
            return carry

        lax.fori_loop(0, count, one, 0)

    edge_spans = ((0, EDGE), (rows - EDGE, rows))
    inner_spans = ((EDGE, rows - EDGE),)

    def first_halo(d, r, at):
        return mid_halo[d, r, :, at]

    def second_halo(d, r, at):
        return halo_ref[1, d, r, :, at]

    def into_state(row, j, v):
        state_ref[row, :, pl.ds(pl.multiple_of(j * unit, unit), unit)] = v

    def into_out(row, j, v):
        out_ref[row, :, pl.ds(pl.multiple_of(j * unit, unit), unit)] = v

    def chemistry(blocks):
        def gather(ref):
            return jnp.concatenate([ref[row, :, t * unit : (t + 1) * unit] for row, t in blocks], 1)

        q = gather(state_ref)
        sun = gather(sun_ref)
        loss = loss_ref[...]
        for _ in range(CHEM):
            high = q.astype(jnp.bfloat16)
            rest = (q - high.astype(jnp.float32)).astype(jnp.bfloat16)
            both = jnp.dot(
                w_ref[...],
                jnp.concatenate([high, rest, high], 0),
                preferred_element_type=jnp.float32,
            )
            q = (q + both[:species] + sun * both[species:]) / (1.0 + loss * q * q)
        spots = range(len(blocks))
        q = jnp.concatenate([q[:, t * unit : (t + 1) * unit] for t in spots], 0)
        high = q.astype(jnp.bfloat16)
        rest = (q - high.astype(jnp.float32)).astype(jnp.bfloat16)
        terms = jnp.concatenate([high, rest, high], 1)
        mixed = [None for t in spots]
        for n in range(0, KMAX, 2):
            both = jnp.dot(
                terms,
                power_ref[:, n * unit : (n + 2) * unit],
                preferred_element_type=jnp.float32,
            )
            for t, (row, place) in enumerate(blocks):
                held = slice(t * species, (t + 1) * species)
                count = cnt_ref[row, :, place * unit : (place + 1) * unit]
                v = both[held, :unit]
                if n > 0:
                    v = jnp.where(count > n, v, mixed[t])
                mixed[t] = jnp.where(count > n + 1, both[held, unit:], v)
        for t, (row, place) in enumerate(blocks):
            state_ref[row, :, place * unit : (place + 1) * unit] = mixed[t]

    edge_rows = [r for first, last in edge_spans for r in range(first, last)]

    def edge_chemistry(parts):
        places = [t for first, last in parts for t in range(first, last)]

        def one(i, carry):
            base = i * (rows - EDGE)
            chemistry([(base + r, t) for r in range(EDGE) for t in places])
            return carry

        if len(places) * len(edge_rows) <= tiles:
            chemistry([(r, t) for r in edge_rows for t in places])
        else:
            lax.fori_loop(0, 2, one, 0)

    prepare_rates()
    prepare_columns()
    build_powers(unit, mix_ref, power_ref)
    comp_west.wait_recv()
    lon_planes(comp_ref[0], comp_ref[1], EDGE)
    first_forwards(range(runs // 2))

    @pl.when(has_south)
    def _():
        for copy in comp_up:
            copy.wait_recv()

    @pl.when(has_north)
    def _():
        for copy in comp_down:
            copy.wait_recv()

    lon_planes(comp_ref[2, rows - EDGE :], comp_ref[4, rows - EDGE :], 0)
    lon_planes(comp_ref[3, :EDGE], comp_ref[5, :EDGE], rows + EDGE)
    for n, ref in enumerate((latc_ref, latk_ref)):
        at = slice((n + 2) * cols, (n + 3) * cols)
        spread(comp_ref[0][:, at], into(ref))
        spread(comp_ref[3][:1, at], into(ref, rows))

    for copy in raw_sides:
        copy.wait()
    lon_sweep(rows, raw_view, whole)
    first_forwards(range(runs // 2, runs))

    for i in range(2):
        halo_arrive(0, i)
    corners = [corner_copies(d) for d in range(2)]
    for d in range(2):

        @pl.when(has[d])
        def _():
            for copy in corners[d]:
                copy.start()

    lat_sweep(mid_ref, first_halo, into_state, inner_spans, whole)
    for d in range(2):

        @pl.when(has[d])
        def _():
            for copy in corners[d]:
                copy.wait()

    edge_sides = side_copies(0) + side_copies(1)
    inner_side = side_copies(2)
    late, passed = 0, 0
    for k in range(groups):
        if k > 0:
            for i in (2 * k, 2 * k + 1):
                halo_arrive(0, i)
        parts = ranges(reach, k)
        lon_sweep(2 * EDGE, raw_halo_view, parts)
        lat_sweep(mid_ref, first_halo, into_state, edge_spans, parts)
        edge_chemistry(parts)
        if k == 0:
            for copy in edge_sides:
                copy.start()
        parts = ranges(after, k)
        if parts:
            if passed == 0:
                for copy in edge_sides:
                    copy.wait()
            lon_sweep(2 * EDGE, state_view(0), parts)
            number = 2 * (sum(last - first for first, last in parts) // (2 * RUN))
            for i in range(passed, passed + number):
                halo_start(1, i)
            forwards(1, range(late, passed))
            late, passed = passed, passed + number

    inner = rows - 2 * EDGE

    def inner_chemistry(i, carry):
        chemistry([(i + EDGE, t) for t in range(tiles)])
        return carry

    lax.fori_loop(0, inner // 2, inner_chemistry, 0)
    forwards(1, range(late, runs))
    lax.fori_loop(inner // 2, inner, inner_chemistry, 0)
    for copy in inner_side:
        copy.start()
    for copy in inner_side:
        copy.wait()
    lon_sweep(inner, state_view(EDGE), whole)
    lat_sweep(again_ref, second_halo, into_out, inner_spans, whole)
    for i in range(runs):
        halo_arrive(1, i)
        lat_sweep(again_ref, second_halo, into_out, edge_spans, [(spans[i], spans[i] + RUN)])

    comp_west.wait_send()

    @pl.when(has_north)
    def _():
        for copy in comp_up:
            copy.wait_send()

    @pl.when(has_south)
    def _():
        for copy in comp_down:
            copy.wait_send()

    halo_sent(0)
    halo_sent(1)


def slopes(c, m):
    return jnp.where(c >= 0.0, 0.5 * (1.0 - c), -0.5 * (1.0 + c)) * m


def shards(
    tracers,
    courant,
    switches,
    day_flags,
    diffusion_counts,
    night_rates,
    photo_rates,
    level_light,
    self_loss,
    vertical_mixing,
):
    species, rows, lanes = tracers.shape
    levels = level_light.shape[0]
    cols = courant.shape[2]
    unit = 2 * levels
    tiles = lanes // unit
    runs = tiles // RUN
    f32, i32, bf16 = jnp.float32, jnp.int32, jnp.bfloat16
    block = (rows, species, lanes)
    halo = (2, EDGE, species, lanes)
    dma = pltpu.SemaphoreType.DMA
    out = pl.pallas_call(
        functools.partial(kernel, unit),
        out_shape=jax.ShapeDtypeStruct(block, f32),
        in_specs=[pl.BlockSpec(memory_space=pltpu.VMEM)] * 10,
        out_specs=pl.BlockSpec(memory_space=pltpu.VMEM),
        scratch_shapes=[
            pltpu.VMEM((6, rows, 4 * cols), f32),
            pltpu.VMEM((rows + 2 * EDGE, 1, lanes + unit), f32),
            pltpu.VMEM((rows + 2 * EDGE, 1, lanes + unit), f32),
            pltpu.VMEM((rows + 1, 1, lanes), f32),
            pltpu.VMEM((rows + 1, 1, lanes), f32),
            pltpu.VMEM((rows, 1, lanes), f32),
            pltpu.VMEM((rows, 1, lanes), i32),
            pltpu.VMEM((1, unit), f32),
            pltpu.VMEM((2 * species, 3 * species), bf16),
            pltpu.VMEM((species, 1), f32),
            pltpu.VMEM(block, f32),
            pltpu.VMEM(halo, f32),
            pltpu.VMEM(block, f32),
            pltpu.VMEM(block, f32),
            pltpu.VMEM((2, rows, species, unit), f32),
            pltpu.VMEM((2, 2, EDGE, species, unit), f32),
            pltpu.VMEM((2, rows, species, unit), f32),
            pltpu.VMEM((2,) + halo, f32),
            pltpu.VMEM((2, species, lanes), f32),
            pltpu.VMEM((3 * unit, KMAX * unit), bf16),
            dma((6,)),
            dma((6,)),
            dma((2, 3, 2)),
            dma((2, 3, 2)),
            dma((2, 2)),
            dma((2, 2)),
            dma((2, 2, runs, EDGE)),
            dma((2, 2, runs, EDGE)),
            dma((2, runs)),
            dma((2, runs)),
        ],
        compiler_params=pltpu.CompilerParams(
            collective_id=0, has_side_effects=True, vmem_limit_bytes=48 * 1024 * 1024
        ),
    )(
        jnp.transpose(tracers, (1, 0, 2)),
        courant,
        switches,
        day_flags,
        diffusion_counts,
        night_rates,
        photo_rates,
        level_light[None],
        self_loss[None],
        vertical_mixing[None],
    )
    return jnp.transpose(out, (1, 0, 2))


def solution(mesh):
    grid = P(None, "lat", "lon")
    plane = P("lat", "lon")
    in_specs = (grid, grid, grid, plane, plane, P(), P(), P(), P(), P())
    return jax.shard_map(shards, mesh=mesh, in_specs=in_specs, out_specs=grid, check_vma=False)
```

```python
import functools

import jax
import jax.numpy as jnp
from jax import lax
from jax.experimental import pallas as pl
from jax.experimental.pallas import tpu as pltpu
from jax.sharding import PartitionSpec as P

CHEM = 6
KMAX = 8
EDGE = 2
AHEAD = 4
CHUNK = 4
MESH = pl.DeviceIdType.MESH


def minmod(x, y):
    return jnp.maximum(jnp.minimum(x, y), 0.0) + jnp.minimum(jnp.maximum(x, y), 0.0)


def face_flux(c, coef, aa, a, b, bb):
    pos = c >= 0.0
    x = jnp.where(pos, a - aa, bb - b)
    return c * (jnp.where(pos, a, b) + coef * minmod(x, b - a))


def build_powers(unit, mix_ref, power_ref):
    source = lax.broadcasted_iota(jnp.int32, (unit, unit), 0)
    target = lax.broadcasted_iota(jnp.int32, (unit, unit), 1)
    up = jnp.broadcast_to(mix_ref[...], (unit, unit))
    down = pltpu.roll(up, 1, 1)
    one = jnp.where(source == target, 1.0 - up - down, 0.0)
    one = jnp.where(source == target + 1, up, one)
    one = jnp.where(source == target - 1, down, one)
    powers = {1: one}
    for n in range(2, KMAX + 1):
        half = n // 2
        powers[n] = jnp.dot(
            powers[half],
            powers[n - half],
            precision=lax.Precision.HIGHEST,
            preferred_element_type=jnp.float32,
        )
    for n, power in powers.items():
        at = slice((n - 1) * unit, n * unit)
        top = power.astype(jnp.bfloat16)
        power_ref[:unit, at] = top
        power_ref[unit : 2 * unit, at] = top
        power_ref[2 * unit :, at] = (power - top.astype(jnp.float32)).astype(jnp.bfloat16)


def kernel(
    unit,
    x_ref,
    courant_ref,
    switch_ref,
    day_ref,
    raw_cnt_ref,
    night_ref,
    photo_ref,
    light_ref,
    raw_loss_ref,
    vertical_ref,
    out_ref,
    comp_ref,
    lonc_ref,
    lonk_ref,
    latc_ref,
    latk_ref,
    sun_ref,
    cnt_ref,
    mix_ref,
    w_ref,
    loss_ref,
    mid_ref,
    state_ref,
    again_ref,
    side_raw,
    side_ref,
    halo_ref,
    relay_ref,
    power_ref,
    comp_send,
    comp_recv,
    side_send,
    side_recv,
    halo_send,
    halo_recv,
    relay_recv,
    relay_send,
):
    rows, species, lanes = x_ref.shape
    cols = courant_ref.shape[2]
    tiles = lanes // unit
    inner = rows - 2 * EDGE
    first_runs, second_runs, swept = plan(tiles)
    runs = (len(first_runs), len(second_runs))
    nlon, nlat = lax.axis_size("lon"), lax.axis_size("lat")
    lon, lat = lax.axis_index("lon"), lax.axis_index("lat")
    east, west = lax.rem(lon + 1, nlon), lax.rem(lon + nlon - 1, nlon)
    has_south, has_north = lat > 0, lat < nlat - 1
    has = (has_south, has_north)
    half = nlat // 2
    relayed = nlat > 2 and nlat % 2 == 0
    is_low_mid, is_high_mid = lat == half - 1, lat == half
    is_mid = jnp.logical_or(is_low_mid, is_high_mid)
    is_relay = jnp.logical_or(lat == 0, lat == nlat - 1)
    relay_of = jnp.where(is_low_mid, nlat - 1, 0)
    relay_to = jnp.where(lat == 0, half - 1, half)
    relay_side = jnp.where(lat == 0, 1, 0)

    def lanes_of(first, last):
        return pl.ds(first * unit, (last - first) * unit)

    def run_lanes(phase, i):
        return lanes_of(*(second_runs if phase else first_runs)[i])

    barrier = pltpu.get_barrier_semaphore()

    def greet(to):
        pl.semaphore_signal(barrier, inc=1, device_id=to, device_id_type=MESH)

    for side in (east, west):
        greet({"lon": side})

    @pl.when(has_south)
    def _():
        greet({"lat": lat - 1})

    @pl.when(has_north)
    def _():
        greet({"lat": lat + 1})

    if relayed:

        @pl.when(is_mid)
        def _():
            greet({"lat": relay_of})

        @pl.when(is_relay)
        def _():
            greet({"lat": jnp.where(lat == 0, half, half - 1)})

    c_own = courant_ref[...]
    m_own = switch_ref[...].astype(jnp.float32)
    row_own = lax.broadcasted_iota(jnp.int32, c_own[1].shape, 0)
    c_lat = jnp.where(jnp.logical_and(row_own == 0, lat == 0), 0.0, c_own[1])
    comp_ref[0] = jnp.concatenate(
        [c_own[0], slopes(c_own[0], m_own[0]), c_lat, slopes(c_lat, m_own[1])], 1
    )

    def remote(src, dst, send, recv, to):
        return pltpu.make_async_remote_copy(
            src_ref=src,
            dst_ref=dst,
            send_sem=send,
            recv_sem=recv,
            device_id=to,
            device_id_type=MESH,
        )

    def comp_copy(slot, to):
        return remote(
            comp_ref.at[0], comp_ref.at[slot], comp_send.at[slot], comp_recv.at[slot], to
        )

    comp_west = comp_copy(1, {"lon": west})
    comp_down = comp_copy(2, {"lat": lat - 1})

    side_rows = ((0, EDGE), (rows - EDGE, EDGE), (EDGE, inner))

    def side_copies(turn, part, row=None):
        held = pl.ds(*side_rows[part]) if row is None else pl.ds(row, 1)
        source, target = (state_ref, side_ref) if turn else (x_ref, side_raw)
        pairs = ((tiles - 1, 0, east), (0, 1, west))
        return [
            remote(
                source.at[held, :, lanes_of(tile, tile + 1)],
                target.at[s, held],
                side_send.at[turn, part, s],
                side_recv.at[turn, part, s],
                {"lon": to},
            )
            for tile, s, to in pairs
        ]

    def row_of(phase, row, i):
        return (again_ref if phase else mid_ref).at[row, :, run_lanes(phase, i)]

    def halo_copy(phase, d, i, r):
        row = r if d else rows - EDGE + r
        return remote(
            row_of(phase, row, i),
            halo_ref.at[phase, d, r, :, run_lanes(phase, i)],
            halo_send.at[phase, d, i, r],
            halo_recv.at[phase, d, i, r],
            {"lat": lat - 1 if d else lat + 1},
        )

    def relay_copy(phase, d, i):
        row = 1 if d else rows - 1
        return remote(
            row_of(phase, row, i),
            relay_ref.at[phase, :, run_lanes(phase, i)],
            halo_send.at[phase, d, i, 1],
            relay_recv.at[phase, i],
            {"lat": relay_of},
        )

    def forward_copy(phase, i):
        return remote(
            relay_ref.at[phase, :, run_lanes(phase, i)],
            halo_ref.at[phase, relay_side, 1, :, run_lanes(phase, i)],
            relay_send.at[phase, i],
            halo_recv.at[phase, relay_side, i, 1],
            {"lat": relay_to},
        )

    def halo_start(phase, i):
        if relayed:

            @pl.when(is_low_mid)
            def _():
                relay_copy(phase, 0, i).start()

            @pl.when(is_high_mid)
            def _():
                relay_copy(phase, 1, i).start()

        for d in (1, 0):
            there = has_south if d else has_north
            direct = there
            if relayed:
                direct = jnp.logical_and(there, jnp.logical_not(is_high_mid if d else is_low_mid))

            @pl.when(there)
            def _():
                halo_copy(phase, d, i, 0).start()

            @pl.when(direct)
            def _():
                halo_copy(phase, d, i, 1).start()

    def halo_sent(phase):
        for i in range(runs[phase]):
            for d in range(2):

                @pl.when(has_south if d else has_north)
                def _():
                    for r in range(EDGE):
                        halo_copy(phase, d, i, r).wait_send()

            if relayed:

                @pl.when(is_relay)
                def _():
                    forward_copy(phase, i).wait_send()

    def halo_arrive(phase, i):
        for d in range(2):

            @pl.when(has[d])
            def _():
                for r in range(EDGE):
                    halo_copy(phase, d, i, r).wait_recv()

    def forward(phase, i):
        if relayed:
            relay_copy(phase, 0, i).wait_recv()
            forward_copy(phase, i).start()

    def forwards(phase, some):
        if relayed:

            @pl.when(is_relay)
            def _():
                for i in some:
                    forward(phase, i)

    def first_forwards(some):
        if relayed:

            @pl.when(is_relay)
            def _():
                for i in some:
                    forward(0, i)
                    if i + AHEAD < runs[0]:
                        halo_start(0, i + AHEAD)

    def spread(plane, target, scale=None):
        left = lax.broadcasted_iota(jnp.int32, (plane.shape[0], unit), 1) < unit // 2
        for j in range(tiles):
            a = jnp.broadcast_to(plane[:, 2 * j : 2 * j + 1], left.shape)
            b = jnp.broadcast_to(plane[:, 2 * j + 1 : 2 * j + 2], left.shape)
            v = jnp.where(left, a, b)
            if scale is not None:
                v = v * scale
            for r in range(plane.shape[0]):
                target(r, slice(j * unit, (j + 1) * unit), v[r : r + 1])

    def into(ref, offset=0):
        def put(r, at, v):
            ref[r + offset, :, at] = v

        return put

    def outer_faces():
        for n, ref in enumerate((lonc_ref, lonk_ref)):
            last = jnp.broadcast_to(comp_ref[1][:, n * cols : n * cols + 1], (rows, unit))
            for r in range(rows):
                ref[r, :, lanes:] = last[r : r + 1]

    def prepare_columns():
        mix = vertical_ref[...]
        gap = jnp.zeros((1, 1), jnp.float32)
        mix_ref[...] = jnp.concatenate([mix, gap, mix, gap], 1)
        light = jnp.concatenate([light_ref[...], light_ref[...]], 1)
        spread(day_ref[...].astype(jnp.float32), into(sun_ref), light)
        spread(raw_cnt_ref[...], into(cnt_ref))

    def prepare_rates():
        rates = jnp.concatenate([night_ref[...], photo_ref[...]], 0)
        top = rates.astype(jnp.bfloat16).astype(jnp.float32)
        w_ref[...] = jnp.concatenate([top, top, rates - top], 1).astype(jnp.bfloat16)
        shape = (species, species)
        same = lax.broadcasted_iota(jnp.int32, shape, 0) == lax.broadcasted_iota(jnp.int32, shape, 1)
        spread_loss = jnp.broadcast_to(raw_loss_ref[...], shape)
        loss_ref[...] = jnp.sum(jnp.where(same, spread_loss, 0.0), axis=1, keepdims=True)

    low = lax.broadcasted_iota(jnp.int32, (species, unit), 1) < unit // 2

    def swap(v):
        return pltpu.roll(v, unit // 2, 1)

    def lon_range(tile, store, e, first, last):
        before, here = tile(first - 1), tile(first)
        swapped = swap(here)
        behind = jnp.where(low, swap(before), swapped)
        flux, turned, cell = None, None, None
        for j in range(first, last + 1):
            if j < last:
                later = tile(j + 1)
                later_swapped = swap(later)
                ahead = jnp.where(low, swapped, later_swapped)
            else:
                later, later_swapped, ahead = here, swapped, swapped
            at = slice(j * unit, (j + 1) * unit)
            now = face_flux(lonc_ref[e, :, at], lonk_ref[e, :, at], before, behind, here, ahead)
            now_turned = swap(now)
            if j > first:
                upper = jnp.where(low, turned, now_turned)
                store(slice((j - 1) * unit, j * unit), cell - (upper - flux))
            flux, turned, cell = now, now_turned, here
            before, here, behind, swapped = here, later, ahead, later_swapped

    def lon_sweep(number, view, parts):
        def one(i, carry):
            tile, store, e = view(i)
            for first, last in parts:
                lon_range(tile, store, e, first, last)
            return carry

        lax.fori_loop(0, number, one, 0)

    whole = [(0, tiles)]
    middle, ends = [(1, tiles - 1)], [(0, 1), (tiles - 1, tiles)]

    def picker(inside, left, right):
        def tile(j):
            if j < 0:
                return left()
            if j == tiles:
                return right()
            return inside(j, slice(j * unit, (j + 1) * unit))

        return tile

    edge_rows = [r for first in (0, rows - EDGE) for r in range(first, first + EDGE)]

    def view(source, sides, target, inside):
        def at_row(i):
            row = i + EDGE if inside else i + (i // EDGE) * (rows - 2 * EDGE)
            tile = picker(
                lambda j, at: source[row, :, at],
                lambda: sides[0, row],
                lambda: sides[1, row],
            )

            def store(at, v):
                target[row, :, at] = v

            return tile, store, row

        return at_row

    raw_edge, raw_inner = (view(x_ref, side_raw, mid_ref, n) for n in (False, True))
    state_edge, state_inner = (view(state_ref, side_ref, again_ref, n) for n in (False, True))

    def lat_sweep(source, halo, store, spans, parts):
        def sweep(j):
            at = pl.ds(pl.multiple_of(j * unit, unit), unit)

            def cell(row):
                if row < 0:
                    return halo(0, row + EDGE, at)
                if row >= rows:
                    return halo(1, row - rows, at)
                return source[row, :, at]

            for first, last in spans:
                aa, a, b = cell(first - 2), cell(first - 1), cell(first)
                flux = None
                for row in range(first, last + 1):
                    bb = cell(row + 1)
                    now = face_flux(latc_ref[row, :, at], latk_ref[row, :, at], aa, a, b, bb)
                    if flux is not None:
                        store(row - 1, j, a - (now - flux))
                    flux = now
                    aa, a, b = a, b, bb

        count = sum(last - first for first, last in parts)
        each = count // len(parts)

        def one(t, carry):
            j = t + parts[0][0]
            if len(parts) > 1:
                j = j + (t // each) * (parts[1][0] - parts[0][0] - each)
            sweep(j)
            return carry

        lax.fori_loop(0, count, one, 0)

    edge_spans = ((0, EDGE), (rows - EDGE, rows))
    inner_spans = ((EDGE, rows - EDGE),)

    def first_halo(d, r, at):
        return halo_ref[0, d, r, :, at]

    def second_halo(d, r, at):
        return halo_ref[1, d, r, :, at]

    def into_state(row, j, v):
        state_ref[row, :, pl.ds(pl.multiple_of(j * unit, unit), unit)] = v

    def into_out(row, j, v):
        out_ref[row, :, pl.ds(pl.multiple_of(j * unit, unit), unit)] = v

    def chemistry(chunks):
        loss = loss_ref[...]

        def react(n, carry):
            for row, spans in chunks:
                for first, last in spans:
                    at = slice(first * unit, last * unit)
                    q = state_ref[row, :, at]
                    high = q.astype(jnp.bfloat16)
                    rest = (q - high.astype(jnp.float32)).astype(jnp.bfloat16)
                    both = jnp.dot(
                        w_ref[...],
                        jnp.concatenate([high, rest, high], 0),
                        preferred_element_type=jnp.float32,
                    )
                    top = q + both[:species] + sun_ref[row, :, at] * both[species:]
                    state_ref[row, :, at] = top / (1.0 + loss * q * q)
            return carry

        lax.fori_loop(0, CHEM, react, 0)
        for row, spans in chunks:
            places = [slice(t * unit, (t + 1) * unit) for span in spans for t in range(*span)]
            q = jnp.concatenate([state_ref[row, :, at] for at in places], 0)
            high = q.astype(jnp.bfloat16)
            rest = (q - high.astype(jnp.float32)).astype(jnp.bfloat16)
            terms = jnp.concatenate([high, rest, high], 1)
            mixed = [None for at in places]
            for n in range(0, KMAX, 2):
                both = jnp.dot(
                    terms,
                    power_ref[:, n * unit : (n + 2) * unit],
                    preferred_element_type=jnp.float32,
                )
                for t, at in enumerate(places):
                    held = slice(t * species, (t + 1) * species)
                    count = cnt_ref[row, :, at]
                    v = both[held, :unit]
                    if n > 0:
                        v = jnp.where(count > n, v, mixed[t])
                    mixed[t] = jnp.where(count > n + 1, both[held, unit:], v)
            for t, at in enumerate(places):
                state_ref[row, :, at] = mixed[t]

    def inner_chunks(row):
        return [(row, [(t, min(t + CHUNK, tiles))]) for t in range(0, tiles, CHUNK)]

    for n, ref in enumerate((lonc_ref, lonk_ref)):
        spread(comp_ref[0][:, n * cols : (n + 1) * cols], into(ref))
    lon_sweep(2 * EDGE, raw_edge, middle)
    for d in range(2):

        @pl.when(jnp.logical_not(has[d]))
        def _():
            for p in range(2):
                halo_ref[p, d] = jnp.zeros(halo_ref.shape[2:], jnp.float32)
            if d:
                comp_ref[2] = jnp.zeros(comp_ref.shape[1:], jnp.float32)

    peers = 2 + jnp.where(has_south, 1, 0) + jnp.where(has_north, 1, 0)
    if relayed:
        peers = peers + jnp.where(jnp.logical_or(is_mid, is_relay), 1, 0)
    pl.semaphore_wait(barrier, peers)

    comp_west.start()

    @pl.when(has_south)
    def _():
        comp_down.start()

    raw_sides = [side_copies(0, part) for part in range(3)]
    for pair in raw_sides:
        for copy in pair:
            copy.start()
    for i in range(2):
        halo_start(0, i)

    prepare_rates()
    prepare_columns()
    build_powers(unit, mix_ref, power_ref)
    for n, ref in enumerate((latc_ref, latk_ref)):
        spread(comp_ref[0][:, (n + 2) * cols : (n + 3) * cols], into(ref))
    comp_west.wait_recv()
    outer_faces()
    for pair in raw_sides[:2]:
        for copy in pair:
            copy.wait()
    lon_sweep(2 * EDGE, raw_edge, ends)
    for i in range(2, AHEAD):
        halo_start(0, i)
    others = True
    if relayed:
        others = jnp.logical_not(is_relay)

    @pl.when(others)
    def _():
        for i in range(AHEAD, runs[0]):
            halo_start(0, i)

    first_forwards(range(2))
    for copy in raw_sides[2]:
        copy.wait()
    lon_sweep(inner, raw_inner, whole)
    first_forwards(range(2, AHEAD))

    @pl.when(has_north)
    def _():
        comp_down.wait_recv()

    for n, ref in enumerate((latc_ref, latk_ref)):
        spread(comp_ref[2][:1, (n + 2) * cols : (n + 3) * cols], into(ref, rows))
    lat_sweep(mid_ref, first_halo, into_state, inner_spans, whole)

    edge_sides = side_copies(1, 0) + side_copies(1, 1)
    ready, late, passed = AHEAD, 0, 0
    for k, parts in enumerate(swept):
        first_forwards(range(ready, min(ready + 2, runs[0])))
        ready += 2
        held = first_runs[2 * k : 2 * k + 2]
        for i in (2 * k, 2 * k + 1):
            halo_arrive(0, i)
        lat_sweep(mid_ref, first_halo, into_state, edge_spans, held)
        chunks = [(row, held) for row in edge_rows]
        if k < inner:
            chunks += inner_chunks(k + EDGE)
        chemistry(chunks)
        if k == 1:
            for copy in edge_sides:
                copy.start()
        if k < inner:
            for copy in side_copies(1, k + 2, k + EDGE):
                copy.start()
        if k == len(swept) - 1:
            for copy in edge_sides:
                copy.wait()
        if parts:
            lon_sweep(2 * EDGE, state_edge, parts)
        number = sum(1 for run in second_runs if any(a <= run[0] < b for a, b in parts))
        for i in range(passed, passed + number):
            halo_start(1, i)
        forwards(1, range(late, passed))
        late, passed = passed, passed + number

    for k in range(len(swept), inner):
        chemistry(inner_chunks(k + EDGE))
        for copy in side_copies(1, k + 2, k + EDGE):
            copy.start()
    for k in range(inner):
        for copy in side_copies(1, k + 2, k + EDGE):
            copy.wait()
    lon_sweep(inner, state_inner, whole)
    forwards(1, range(late, runs[1]))
    lat_sweep(again_ref, second_halo, into_out, inner_spans, whole)
    for i in range(runs[1]):
        halo_arrive(1, i)
        lat_sweep(again_ref, second_halo, into_out, edge_spans, [second_runs[i]])

    comp_west.wait_send()

    @pl.when(has_south)
    def _():
        comp_down.wait_send()

    halo_sent(0)
    halo_sent(1)


def plan(tiles):
    pairs = tiles // 4
    order = [1, 0, *range(2, pairs)]
    first = [run for p in order for run in ((2 * p, 2 * p + 2), (tiles - 2 * p - 2, tiles - 2 * p))]
    swept = [[], [(1, 3), (tiles - 3, tiles - 1)]]
    for p in range(2, pairs - 1):
        swept.append([(2 * p - 1, 2 * p + 1), (tiles - 2 * p - 1, tiles - 2 * p + 1)])
    last = 2 * pairs - 3
    swept.append([(last, tiles - last), (0, 1), (tiles - 1, tiles)])
    second = []
    for parts in swept:
        for a, b in parts:
            second += [(t, min(t + 2, b)) for t in range(a, b, 2)]
    return first, second, swept


def slopes(c, m):
    return jnp.where(c >= 0.0, 0.5 * (1.0 - c), -0.5 * (1.0 + c)) * m


def shards(
    tracers,
    courant,
    switches,
    day_flags,
    diffusion_counts,
    night_rates,
    photo_rates,
    level_light,
    self_loss,
    vertical_mixing,
):
    species, rows, lanes = tracers.shape
    levels = level_light.shape[0]
    cols = courant.shape[2]
    unit = 2 * levels
    tiles = lanes // unit
    runs = max(len(part) for part in plan(tiles)[:2])
    f32, i32, bf16 = jnp.float32, jnp.int32, jnp.bfloat16
    block = (rows, species, lanes)
    halo = (2, EDGE, species, lanes)
    dma = pltpu.SemaphoreType.DMA
    out = pl.pallas_call(
        functools.partial(kernel, unit),
        out_shape=jax.ShapeDtypeStruct(block, f32),
        in_specs=[pl.BlockSpec(memory_space=pltpu.VMEM)] * 10,
        out_specs=pl.BlockSpec(memory_space=pltpu.VMEM),
        scratch_shapes=[
            pltpu.VMEM((3, rows, 4 * cols), f32),
            pltpu.VMEM((rows, 1, lanes + unit), f32),
            pltpu.VMEM((rows, 1, lanes + unit), f32),
            pltpu.VMEM((rows + 1, 1, lanes), f32),
            pltpu.VMEM((rows + 1, 1, lanes), f32),
            pltpu.VMEM((rows, 1, lanes), f32),
            pltpu.VMEM((rows, 1, lanes), i32),
            pltpu.VMEM((1, unit), f32),
            pltpu.VMEM((2 * species, 3 * species), bf16),
            pltpu.VMEM((species, 1), f32),
            pltpu.VMEM(block, f32),
            pltpu.VMEM(block, f32),
            pltpu.VMEM(block, f32),
            pltpu.VMEM((2, rows, species, unit), f32),
            pltpu.VMEM((2, rows, species, unit), f32),
            pltpu.VMEM((2,) + halo, f32),
            pltpu.VMEM((2, species, lanes), f32),
            pltpu.VMEM((3 * unit, KMAX * unit), bf16),
            dma((3,)),
            dma((3,)),
            dma((2, rows, 2)),
            dma((2, rows, 2)),
            dma((2, 2, runs, EDGE)),
            dma((2, 2, runs, EDGE)),
            dma((2, runs)),
            dma((2, runs)),
        ],
        compiler_params=pltpu.CompilerParams(
            collective_id=0, has_side_effects=True, vmem_limit_bytes=48 * 1024 * 1024
        ),
    )(
        jnp.transpose(tracers, (1, 0, 2)),
        courant,
        switches,
        day_flags,
        diffusion_counts,
        night_rates,
        photo_rates,
        level_light[None],
        self_loss[None],
        vertical_mixing[None],
    )
    return jnp.transpose(out, (1, 0, 2))


def solution(mesh):
    grid = P(None, "lat", "lon")
    plane = P("lat", "lon")
    in_specs = (grid, grid, grid, plane, plane, P(), P(), P(), P(), P())
    return jax.shard_map(shards, mesh=mesh, in_specs=in_specs, out_specs=grid, check_vma=False)
```

```python
import functools

import jax
import jax.numpy as jnp
from jax import lax
from jax.experimental import pallas as pl
from jax.experimental.pallas import tpu as pltpu
from jax.sharding import PartitionSpec as P

CHEM = 6
KMAX = 8
EDGE = 2
AHEAD = 2
CHUNK = 4
BESIDE = (2, 1, 1)
MESH = pl.DeviceIdType.MESH


def minmod(x, y):
    return jnp.maximum(jnp.minimum(x, y), 0.0) + jnp.minimum(jnp.maximum(x, y), 0.0)


def face_flux(c, coef, aa, a, b, bb):
    pos = c >= 0.0
    x = jnp.where(pos, a - aa, bb - b)
    return c * (jnp.where(pos, a, b) + coef * minmod(x, b - a))


def build_powers(unit, mix_ref, power_ref):
    source = lax.broadcasted_iota(jnp.int32, (unit, unit), 0)
    target = lax.broadcasted_iota(jnp.int32, (unit, unit), 1)
    up = jnp.broadcast_to(mix_ref[...], (unit, unit))
    down = pltpu.roll(up, 1, 1)
    one = jnp.where(source == target, 1.0 - up - down, 0.0)
    one = jnp.where(source == target + 1, up, one)
    one = jnp.where(source == target - 1, down, one)
    powers = {1: one}
    for n in range(2, KMAX + 1):
        half = n // 2
        powers[n] = jnp.dot(
            powers[half],
            powers[n - half],
            precision=lax.Precision.HIGHEST,
            preferred_element_type=jnp.float32,
        )
    for n, power in powers.items():
        at = slice((n - 1) * unit, n * unit)
        top = power.astype(jnp.bfloat16)
        power_ref[:unit, at] = top
        power_ref[unit : 2 * unit, at] = top
        power_ref[2 * unit :, at] = (power - top.astype(jnp.float32)).astype(jnp.bfloat16)


def kernel(
    unit,
    x_ref,
    courant_ref,
    switch_ref,
    day_ref,
    raw_cnt_ref,
    night_ref,
    photo_ref,
    light_ref,
    raw_loss_ref,
    vertical_ref,
    out_ref,
    comp_ref,
    lonc_ref,
    lonk_ref,
    latc_ref,
    latk_ref,
    sun_ref,
    cnt_ref,
    mix_ref,
    w_ref,
    loss_ref,
    mid_ref,
    state_ref,
    again_ref,
    side_raw,
    side_ref,
    halo_ref,
    relay_ref,
    power_ref,
    comp_send,
    comp_recv,
    side_send,
    side_recv,
    halo_send,
    halo_recv,
    relay_recv,
    relay_send,
):
    rows, species, lanes = x_ref.shape
    cols = courant_ref.shape[2]
    tiles = lanes // unit
    inner = rows - 2 * EDGE
    first_runs, second_runs, swept = plan(tiles)
    runs = (len(first_runs), len(second_runs))
    nlon, nlat = lax.axis_size("lon"), lax.axis_size("lat")
    lon, lat = lax.axis_index("lon"), lax.axis_index("lat")
    east, west = lax.rem(lon + 1, nlon), lax.rem(lon + nlon - 1, nlon)
    has_south, has_north = lat > 0, lat < nlat - 1
    has = (has_south, has_north)
    half = nlat // 2
    relayed = nlat > 2 and nlat % 2 == 0
    is_low_mid, is_high_mid = lat == half - 1, lat == half
    is_mid = jnp.logical_or(is_low_mid, is_high_mid)
    is_relay = jnp.logical_or(lat == 0, lat == nlat - 1)
    relay_of = jnp.where(is_low_mid, nlat - 1, 0)
    relay_to = jnp.where(lat == 0, half - 1, half)
    relay_side = jnp.where(lat == 0, 1, 0)

    def lanes_of(first, last):
        return pl.ds(first * unit, (last - first) * unit)

    def run_lanes(phase, i):
        return lanes_of(*(second_runs if phase else first_runs)[i])

    barrier = pltpu.get_barrier_semaphore()

    def greet(to):
        pl.semaphore_signal(barrier, inc=1, device_id=to, device_id_type=MESH)

    for side in (east, west):
        greet({"lon": side})

    @pl.when(has_south)
    def _():
        greet({"lat": lat - 1})

    @pl.when(has_north)
    def _():
        greet({"lat": lat + 1})

    if relayed:

        @pl.when(is_mid)
        def _():
            greet({"lat": relay_of})

        @pl.when(is_relay)
        def _():
            greet({"lat": jnp.where(lat == 0, half, half - 1)})

    c_own = courant_ref[...]
    m_own = switch_ref[...].astype(jnp.float32)
    row_own = lax.broadcasted_iota(jnp.int32, c_own[1].shape, 0)
    c_lat = jnp.where(jnp.logical_and(row_own == 0, lat == 0), 0.0, c_own[1])
    comp_ref[0] = jnp.concatenate(
        [c_own[0], slopes(c_own[0], m_own[0]), c_lat, slopes(c_lat, m_own[1])], 1
    )

    def remote(src, dst, send, recv, to):
        return pltpu.make_async_remote_copy(
            src_ref=src,
            dst_ref=dst,
            send_sem=send,
            recv_sem=recv,
            device_id=to,
            device_id_type=MESH,
        )

    def comp_copy(slot, to):
        return remote(
            comp_ref.at[0], comp_ref.at[slot], comp_send.at[slot], comp_recv.at[slot], to
        )

    comp_west = comp_copy(1, {"lon": west})
    comp_down = comp_copy(2, {"lat": lat - 1})

    side_rows = ((0, EDGE), (rows - EDGE, EDGE), (EDGE, inner))

    def side_copies(turn, part, row=None):
        held = pl.ds(*side_rows[part]) if row is None else pl.ds(row, 1)
        source, target = (state_ref, side_ref) if turn else (x_ref, side_raw)
        pairs = ((tiles - 1, 0, east), (0, 1, west))
        return [
            remote(
                source.at[held, :, lanes_of(tile, tile + 1)],
                target.at[s, held],
                side_send.at[turn, part, s],
                side_recv.at[turn, part, s],
                {"lon": to},
            )
            for tile, s, to in pairs
        ]

    def row_of(phase, row, i):
        return (again_ref if phase else mid_ref).at[row, :, run_lanes(phase, i)]

    def halo_copy(phase, d, i, r):
        row = r if d else rows - EDGE + r
        return remote(
            row_of(phase, row, i),
            halo_ref.at[phase, d, r, :, run_lanes(phase, i)],
            halo_send.at[phase, d, i, r],
            halo_recv.at[phase, d, i, r],
            {"lat": lat - 1 if d else lat + 1},
        )

    def relay_copy(phase, d, i):
        row = 1 if d else rows - 1
        return remote(
            row_of(phase, row, i),
            relay_ref.at[phase, :, run_lanes(phase, i)],
            halo_send.at[phase, d, i, 1],
            relay_recv.at[phase, i],
            {"lat": relay_of},
        )

    def forward_copy(phase, i):
        return remote(
            relay_ref.at[phase, :, run_lanes(phase, i)],
            halo_ref.at[phase, relay_side, 1, :, run_lanes(phase, i)],
            relay_send.at[phase, i],
            halo_recv.at[phase, relay_side, i, 1],
            {"lat": relay_to},
        )

    def halo_start(phase, i):
        if relayed:

            @pl.when(is_low_mid)
            def _():
                relay_copy(phase, 0, i).start()

            @pl.when(is_high_mid)
            def _():
                relay_copy(phase, 1, i).start()

        for d in (1, 0):
            there = has_south if d else has_north
            direct = there
            if relayed:
                direct = jnp.logical_and(there, jnp.logical_not(is_high_mid if d else is_low_mid))

            @pl.when(there)
            def _():
                halo_copy(phase, d, i, 0).start()

            @pl.when(direct)
            def _():
                halo_copy(phase, d, i, 1).start()

    def halo_sent(phase):
        for i in range(runs[phase]):
            for d in range(2):

                @pl.when(has_south if d else has_north)
                def _():
                    for r in range(EDGE):
                        halo_copy(phase, d, i, r).wait_send()

            if relayed:

                @pl.when(is_relay)
                def _():
                    forward_copy(phase, i).wait_send()

    def halo_arrive(phase, i):
        for d in range(2):

            @pl.when(has[d])
            def _():
                for r in range(EDGE):
                    halo_copy(phase, d, i, r).wait_recv()

    def forward(phase, i):
        if relayed:
            relay_copy(phase, 0, i).wait_recv()
            forward_copy(phase, i).start()

    def forwards(phase, some):
        if relayed:

            @pl.when(is_relay)
            def _():
                for i in some:
                    forward(phase, i)

    def first_forwards(some):
        if relayed:

            @pl.when(is_relay)
            def _():
                for i in some:
                    forward(0, i)
                    if i + AHEAD < runs[0]:
                        halo_start(0, i + AHEAD)

    def spread(plane, target, scale=None):
        left = lax.broadcasted_iota(jnp.int32, (plane.shape[0], unit), 1) < unit // 2
        for j in range(tiles):
            a = jnp.broadcast_to(plane[:, 2 * j : 2 * j + 1], left.shape)
            b = jnp.broadcast_to(plane[:, 2 * j + 1 : 2 * j + 2], left.shape)
            v = jnp.where(left, a, b)
            if scale is not None:
                v = v * scale
            for r in range(plane.shape[0]):
                target(r, slice(j * unit, (j + 1) * unit), v[r : r + 1])

    def into(ref, offset=0):
        def put(r, at, v):
            ref[r + offset, :, at] = v

        return put

    def outer_faces():
        for n, ref in enumerate((lonc_ref, lonk_ref)):
            last = jnp.broadcast_to(comp_ref[1][:, n * cols : n * cols + 1], (rows, unit))
            for r in range(rows):
                ref[r, :, lanes:] = last[r : r + 1]

    def prepare_columns():
        mix = vertical_ref[...]
        gap = jnp.zeros((1, 1), jnp.float32)
        mix_ref[...] = jnp.concatenate([mix, gap, mix, gap], 1)
        light = jnp.concatenate([light_ref[...], light_ref[...]], 1)
        spread(day_ref[...].astype(jnp.float32), into(sun_ref), light)
        spread(raw_cnt_ref[...], into(cnt_ref))

    def prepare_rates():
        rates = jnp.concatenate([night_ref[...], photo_ref[...]], 0)
        top = rates.astype(jnp.bfloat16).astype(jnp.float32)
        w_ref[...] = jnp.concatenate([top, top, rates - top], 1).astype(jnp.bfloat16)
        shape = (species, species)
        same = lax.broadcasted_iota(jnp.int32, shape, 0) == lax.broadcasted_iota(jnp.int32, shape, 1)
        spread_loss = jnp.broadcast_to(raw_loss_ref[...], shape)
        loss_ref[...] = jnp.sum(jnp.where(same, spread_loss, 0.0), axis=1, keepdims=True)

    low = lax.broadcasted_iota(jnp.int32, (species, unit), 1) < unit // 2

    def swap(v):
        return pltpu.roll(v, unit // 2, 1)

    def lon_range(tile, store, e, first, last):
        before, here = tile(first - 1), tile(first)
        swapped = swap(here)
        behind = jnp.where(low, swap(before), swapped)
        flux, turned, cell = None, None, None
        for j in range(first, last + 1):
            if j < last:
                later = tile(j + 1)
                later_swapped = swap(later)
                ahead = jnp.where(low, swapped, later_swapped)
            else:
                later, later_swapped, ahead = here, swapped, swapped
            at = slice(j * unit, (j + 1) * unit)
            now = face_flux(lonc_ref[e, :, at], lonk_ref[e, :, at], before, behind, here, ahead)
            now_turned = swap(now)
            if j > first:
                upper = jnp.where(low, turned, now_turned)
                store(slice((j - 1) * unit, j * unit), cell - (upper - flux))
            flux, turned, cell = now, now_turned, here
            before, here, behind, swapped = here, later, ahead, later_swapped

    def lon_sweep(number, view, parts):
        def one(i, carry):
            tile, store, e = view(i)
            for first, last in parts:
                lon_range(tile, store, e, first, last)
            return carry

        lax.fori_loop(0, number, one, 0)

    whole = [(0, tiles)]
    middle, ends = [(1, tiles - 1)], [(0, 1), (tiles - 1, tiles)]

    def picker(inside, left, right):
        def tile(j):
            if j < 0:
                return left()
            if j == tiles:
                return right()
            return inside(j, slice(j * unit, (j + 1) * unit))

        return tile

    edge_rows = [r for first in (0, rows - EDGE) for r in range(first, first + EDGE)]

    def view(source, sides, target, inside):
        def at_row(i):
            row = i + EDGE if inside else i + (i // EDGE) * (rows - 2 * EDGE)
            tile = picker(
                lambda j, at: source[row, :, at],
                lambda: sides[0, row],
                lambda: sides[1, row],
            )

            def store(at, v):
                target[row, :, at] = v

            return tile, store, row

        return at_row

    raw_edge, raw_inner = (view(x_ref, side_raw, mid_ref, n) for n in (False, True))
    state_edge, state_inner = (view(state_ref, side_ref, again_ref, n) for n in (False, True))

    def lat_sweep(source, halo, store, spans, parts):
        def sweep(j):
            at = pl.ds(pl.multiple_of(j * unit, unit), unit)

            def cell(row):
                if row < 0:
                    return halo(0, row + EDGE, at)
                if row >= rows:
                    return halo(1, row - rows, at)
                return source[row, :, at]

            for first, last in spans:
                aa, a, b = cell(first - 2), cell(first - 1), cell(first)
                flux = None
                for row in range(first, last + 1):
                    bb = cell(row + 1)
                    now = face_flux(latc_ref[row, :, at], latk_ref[row, :, at], aa, a, b, bb)
                    if flux is not None:
                        store(row - 1, j, a - (now - flux))
                    flux = now
                    aa, a, b = a, b, bb

        count = sum(last - first for first, last in parts)
        each = count // len(parts)

        def one(t, carry):
            j = t + parts[0][0]
            if len(parts) > 1:
                j = j + (t // each) * (parts[1][0] - parts[0][0] - each)
            sweep(j)
            return carry

        lax.fori_loop(0, count, one, 0)

    edge_spans = ((0, EDGE), (rows - EDGE, rows))
    inner_spans = ((EDGE, rows - EDGE),)

    def first_halo(d, r, at):
        return halo_ref[0, d, r, :, at]

    def second_halo(d, r, at):
        return halo_ref[1, d, r, :, at]

    def into_state(row, j, v):
        state_ref[row, :, pl.ds(pl.multiple_of(j * unit, unit), unit)] = v

    def into_out(row, j, v):
        out_ref[row, :, pl.ds(pl.multiple_of(j * unit, unit), unit)] = v

    def chemistry(chunks):
        loss = loss_ref[...]

        def react(n, carry):
            for row, spans in chunks:
                for first, last in spans:
                    at = slice(first * unit, last * unit)
                    q = state_ref[row, :, at]
                    high = q.astype(jnp.bfloat16)
                    rest = (q - high.astype(jnp.float32)).astype(jnp.bfloat16)
                    both = jnp.dot(
                        w_ref[...],
                        jnp.concatenate([high, rest, high], 0),
                        preferred_element_type=jnp.float32,
                    )
                    top = q + both[:species] + sun_ref[row, :, at] * both[species:]
                    state_ref[row, :, at] = top / (1.0 + loss * q * q)
            return carry

        lax.fori_loop(0, CHEM, react, 0)
        for row, spans in chunks:
            places = [slice(t * unit, (t + 1) * unit) for span in spans for t in range(*span)]
            q = jnp.concatenate([state_ref[row, :, at] for at in places], 0)
            high = q.astype(jnp.bfloat16)
            rest = (q - high.astype(jnp.float32)).astype(jnp.bfloat16)
            terms = jnp.concatenate([high, rest, high], 1)
            mixed = [None for at in places]
            for n in range(0, KMAX, 2):
                both = jnp.dot(
                    terms,
                    power_ref[:, n * unit : (n + 2) * unit],
                    preferred_element_type=jnp.float32,
                )
                for t, at in enumerate(places):
                    held = slice(t * species, (t + 1) * species)
                    count = cnt_ref[row, :, at]
                    v = both[held, :unit]
                    if n > 0:
                        v = jnp.where(count > n, v, mixed[t])
                    mixed[t] = jnp.where(count > n + 1, both[held, unit:], v)
            for t, at in enumerate(places):
                state_ref[row, :, at] = mixed[t]

    def inner_chunks(row):
        return [(row, [(t, min(t + CHUNK, tiles))]) for t in range(0, tiles, CHUNK)]

    for n, ref in enumerate((lonc_ref, lonk_ref)):
        spread(comp_ref[0][:, n * cols : (n + 1) * cols], into(ref))
    lon_sweep(2 * EDGE, raw_edge, middle)
    for d in range(2):

        @pl.when(jnp.logical_not(has[d]))
        def _():
            for p in range(2):
                halo_ref[p, d] = jnp.zeros(halo_ref.shape[2:], jnp.float32)
            if d:
                comp_ref[2] = jnp.zeros(comp_ref.shape[1:], jnp.float32)

    peers = 2 + jnp.where(has_south, 1, 0) + jnp.where(has_north, 1, 0)
    if relayed:
        peers = peers + jnp.where(jnp.logical_or(is_mid, is_relay), 1, 0)
    pl.semaphore_wait(barrier, peers)

    comp_west.start()

    @pl.when(has_south)
    def _():
        comp_down.start()

    raw_sides = [side_copies(0, part) for part in range(3)]
    for pair in raw_sides:
        for copy in pair:
            copy.start()
    for i in range(2):
        halo_start(0, i)

    prepare_rates()
    prepare_columns()
    build_powers(unit, mix_ref, power_ref)
    for n, ref in enumerate((latc_ref, latk_ref)):
        spread(comp_ref[0][:, (n + 2) * cols : (n + 3) * cols], into(ref))
    comp_west.wait_recv()
    outer_faces()
    for pair in raw_sides[:2]:
        for copy in pair:
            copy.wait()
    lon_sweep(2 * EDGE, raw_edge, ends)
    for i in range(2, max(AHEAD, 2)):
        halo_start(0, i)
    others = True
    if relayed:
        others = jnp.logical_not(is_relay)

    @pl.when(others)
    def _():
        for i in range(max(AHEAD, 2), runs[0]):
            halo_start(0, i)

    first_forwards(range(2))
    for copy in raw_sides[2]:
        copy.wait()
    lon_sweep(inner, raw_inner, whole)

    @pl.when(has_north)
    def _():
        comp_down.wait_recv()

    for n, ref in enumerate((latc_ref, latk_ref)):
        spread(comp_ref[2][:1, (n + 2) * cols : (n + 3) * cols], into(ref, rows))
    lat_sweep(mid_ref, first_halo, into_state, inner_spans, whole)

    edge_sides = side_copies(1, 0) + side_copies(1, 1)
    ready, late, passed, done = 2, 0, 0, 0
    for k, parts in enumerate(swept):
        first_forwards(range(ready, min(ready + 2, runs[0])))
        ready += 2
        held = first_runs[2 * k : 2 * k + 2]
        for i in (2 * k, 2 * k + 1):
            halo_arrive(0, i)
        lat_sweep(mid_ref, first_halo, into_state, edge_spans, held)
        chunks = [(row, held) for row in edge_rows]
        beside = range(done, min(done + (BESIDE + (0,) * k)[k], inner))
        for i in beside:
            chunks += inner_chunks(i + EDGE)
        chemistry(chunks)
        if k == 1:
            for copy in edge_sides:
                copy.start()
        for i in beside:
            for copy in side_copies(1, i + 2, i + EDGE):
                copy.start()
        done += len(beside)
        if k == 2:
            for copy in edge_sides:
                copy.wait()
        forwards(1, range(late, passed))
        if parts:
            lon_sweep(2 * EDGE, state_edge, parts)
        number = sum(1 for run in second_runs if any(a <= run[0] < b for a, b in parts))
        for i in range(passed, passed + number):
            halo_start(1, i)
        late, passed = passed, passed + number

    for k in range(done, inner):
        chemistry(inner_chunks(k + EDGE))
        for copy in side_copies(1, k + 2, k + EDGE):
            copy.start()
    for k in range(inner):
        for copy in side_copies(1, k + 2, k + EDGE):
            copy.wait()
    lon_sweep(inner, state_inner, whole)
    forwards(1, range(late, runs[1]))
    lat_sweep(again_ref, second_halo, into_out, inner_spans, whole)
    for i in range(runs[1]):
        halo_arrive(1, i)
        lat_sweep(again_ref, second_halo, into_out, edge_spans, [second_runs[i]])

    comp_west.wait_send()

    @pl.when(has_south)
    def _():
        comp_down.wait_send()

    halo_sent(0)
    halo_sent(1)


def plan(tiles):
    pairs = tiles // 4
    order = [1, 0, *range(2, pairs)]
    first = [run for p in order for run in ((2 * p, 2 * p + 2), (tiles - 2 * p - 2, tiles - 2 * p))]
    swept = [[], [(1, 3), (tiles - 3, tiles - 1)]]
    for p in range(2, pairs):
        swept.append([(2 * p - 1, 2 * p + 1), (tiles - 2 * p - 1, tiles - 2 * p + 1)])
    swept[-1] = [(2 * pairs - 3, tiles - 2 * pairs + 3)]
    swept[2] = swept[2] + [(0, 1), (tiles - 1, tiles)]
    second = []
    for parts in swept:
        for a, b in parts:
            second += [(t, min(t + 2, b)) for t in range(a, b, 2)]
    return first, second, swept


def slopes(c, m):
    return jnp.where(c >= 0.0, 0.5 * (1.0 - c), -0.5 * (1.0 + c)) * m


def shards(
    tracers,
    courant,
    switches,
    day_flags,
    diffusion_counts,
    night_rates,
    photo_rates,
    level_light,
    self_loss,
    vertical_mixing,
):
    species, rows, lanes = tracers.shape
    levels = level_light.shape[0]
    cols = courant.shape[2]
    unit = 2 * levels
    tiles = lanes // unit
    runs = max(len(part) for part in plan(tiles)[:2])
    f32, i32, bf16 = jnp.float32, jnp.int32, jnp.bfloat16
    block = (rows, species, lanes)
    halo = (2, EDGE, species, lanes)
    dma = pltpu.SemaphoreType.DMA
    out = pl.pallas_call(
        functools.partial(kernel, unit),
        out_shape=jax.ShapeDtypeStruct(block, f32),
        in_specs=[pl.BlockSpec(memory_space=pltpu.VMEM)] * 10,
        out_specs=pl.BlockSpec(memory_space=pltpu.VMEM),
        scratch_shapes=[
            pltpu.VMEM((3, rows, 4 * cols), f32),
            pltpu.VMEM((rows, 1, lanes + unit), f32),
            pltpu.VMEM((rows, 1, lanes + unit), f32),
            pltpu.VMEM((rows + 1, 1, lanes), f32),
            pltpu.VMEM((rows + 1, 1, lanes), f32),
            pltpu.VMEM((rows, 1, lanes), f32),
            pltpu.VMEM((rows, 1, lanes), i32),
            pltpu.VMEM((1, unit), f32),
            pltpu.VMEM((2 * species, 3 * species), bf16),
            pltpu.VMEM((species, 1), f32),
            pltpu.VMEM(block, f32),
            pltpu.VMEM(block, f32),
            pltpu.VMEM(block, f32),
            pltpu.VMEM((2, rows, species, unit), f32),
            pltpu.VMEM((2, rows, species, unit), f32),
            pltpu.VMEM((2,) + halo, f32),
            pltpu.VMEM((2, species, lanes), f32),
            pltpu.VMEM((3 * unit, KMAX * unit), bf16),
            dma((3,)),
            dma((3,)),
            dma((2, rows, 2)),
            dma((2, rows, 2)),
            dma((2, 2, runs, EDGE)),
            dma((2, 2, runs, EDGE)),
            dma((2, runs)),
            dma((2, runs)),
        ],
        compiler_params=pltpu.CompilerParams(
            collective_id=0, has_side_effects=True, vmem_limit_bytes=48 * 1024 * 1024
        ),
    )(
        jnp.transpose(tracers, (1, 0, 2)),
        courant,
        switches,
        day_flags,
        diffusion_counts,
        night_rates,
        photo_rates,
        level_light[None],
        self_loss[None],
        vertical_mixing[None],
    )
    return jnp.transpose(out, (1, 0, 2))


def solution(mesh):
    grid = P(None, "lat", "lon")
    plane = P("lat", "lon")
    in_specs = (grid, grid, grid, plane, plane, P(), P(), P(), P(), P())
    return jax.shard_map(shards, mesh=mesh, in_specs=in_specs, out_specs=grid, check_vma=False)
```

```python
import functools

import jax
import jax.numpy as jnp
from jax import lax
from jax.experimental import pallas as pl
from jax.experimental.pallas import tpu as pltpu
from jax.sharding import PartitionSpec as P

CHEM = 6
KMAX = 8
EDGE = 2
AHEAD = 2
CHUNK = 4
BESIDE = (2, 1, 1)
MESH = pl.DeviceIdType.MESH


def minmod(x, y):
    return jnp.maximum(jnp.minimum(x, y), 0.0) + jnp.minimum(jnp.maximum(x, y), 0.0)


def face_flux(c, coef, aa, a, b, bb):
    pos = c >= 0.0
    x = jnp.where(pos, a - aa, bb - b)
    return c * (jnp.where(pos, a, b) + coef * minmod(x, b - a))


def build_powers(unit, mix_ref, power_ref):
    source = lax.broadcasted_iota(jnp.int32, (unit, unit), 0)
    target = lax.broadcasted_iota(jnp.int32, (unit, unit), 1)
    up = jnp.broadcast_to(mix_ref[...], (unit, unit))
    down = pltpu.roll(up, 1, 1)
    one = jnp.where(source == target, 1.0 - up - down, 0.0)
    one = jnp.where(source == target + 1, up, one)
    one = jnp.where(source == target - 1, down, one)
    powers = {1: one}
    for n in range(2, KMAX + 1):
        half = n // 2
        powers[n] = jnp.dot(
            powers[half],
            powers[n - half],
            precision=lax.Precision.HIGHEST,
            preferred_element_type=jnp.float32,
        )
    for n, power in powers.items():
        at = slice((n - 1) * unit, n * unit)
        top = power.astype(jnp.bfloat16)
        power_ref[:unit, at] = top
        power_ref[unit : 2 * unit, at] = top
        power_ref[2 * unit :, at] = (power - top.astype(jnp.float32)).astype(jnp.bfloat16)


def kernel(
    unit,
    x_ref,
    courant_ref,
    switch_ref,
    day_ref,
    raw_cnt_ref,
    night_ref,
    photo_ref,
    light_ref,
    raw_loss_ref,
    vertical_ref,
    out_ref,
    comp_ref,
    lonc_ref,
    lonk_ref,
    latc_ref,
    latk_ref,
    sun_ref,
    cnt_ref,
    mix_ref,
    w_ref,
    loss_ref,
    mid_ref,
    state_ref,
    again_ref,
    side_raw,
    side_ref,
    halo_ref,
    relay_ref,
    power_ref,
    comp_send,
    comp_recv,
    side_send,
    side_recv,
    halo_send,
    halo_recv,
    relay_recv,
    relay_send,
):
    rows, species, lanes = x_ref.shape
    cols = courant_ref.shape[2]
    tiles = lanes // unit
    inner = rows - 2 * EDGE
    first_runs, second_runs, swept = plan(tiles)
    runs = (len(first_runs), len(second_runs))
    nlon, nlat = lax.axis_size("lon"), lax.axis_size("lat")
    lon, lat = lax.axis_index("lon"), lax.axis_index("lat")
    east, west = lax.rem(lon + 1, nlon), lax.rem(lon + nlon - 1, nlon)
    has_south, has_north = lat > 0, lat < nlat - 1
    has = (has_south, has_north)
    half = nlat // 2
    relayed = nlat > 2 and nlat % 2 == 0
    is_low_mid, is_high_mid = lat == half - 1, lat == half
    is_mid = jnp.logical_or(is_low_mid, is_high_mid)
    is_relay = jnp.logical_or(lat == 0, lat == nlat - 1)
    relay_of = jnp.where(is_low_mid, nlat - 1, 0)
    relay_to = jnp.where(lat == 0, half - 1, half)
    relay_side = jnp.where(lat == 0, 1, 0)

    def lanes_of(first, last):
        return pl.ds(first * unit, (last - first) * unit)

    def run_lanes(phase, i):
        return lanes_of(*(second_runs if phase else first_runs)[i])

    barrier = pltpu.get_barrier_semaphore()

    def greet(to):
        pl.semaphore_signal(barrier, inc=1, device_id=to, device_id_type=MESH)

    for side in (east, west):
        greet({"lon": side})

    @pl.when(has_south)
    def _():
        greet({"lat": lat - 1})

    @pl.when(has_north)
    def _():
        greet({"lat": lat + 1})

    if relayed:

        @pl.when(is_mid)
        def _():
            greet({"lat": relay_of})

        @pl.when(is_relay)
        def _():
            greet({"lat": jnp.where(lat == 0, half, half - 1)})

    c_own = courant_ref[...]
    m_own = switch_ref[...].astype(jnp.float32)
    row_own = lax.broadcasted_iota(jnp.int32, c_own[1].shape, 0)
    c_lat = jnp.where(jnp.logical_and(row_own == 0, lat == 0), 0.0, c_own[1])
    comp_ref[0] = jnp.concatenate(
        [c_own[0], slopes(c_own[0], m_own[0]), c_lat, slopes(c_lat, m_own[1])], 1
    )

    def remote(src, dst, send, recv, to):
        return pltpu.make_async_remote_copy(
            src_ref=src,
            dst_ref=dst,
            send_sem=send,
            recv_sem=recv,
            device_id=to,
            device_id_type=MESH,
        )

    def comp_copy(slot, to):
        return remote(
            comp_ref.at[0], comp_ref.at[slot], comp_send.at[slot], comp_recv.at[slot], to
        )

    comp_west = comp_copy(1, {"lon": west})
    comp_down = comp_copy(2, {"lat": lat - 1})

    side_rows = ((0, EDGE), (rows - EDGE, EDGE), (EDGE, inner))

    def side_copies(turn, part, row=None):
        held = pl.ds(*side_rows[part]) if row is None else pl.ds(row, 1)
        source, target = (state_ref, side_ref) if turn else (x_ref, side_raw)
        pairs = ((tiles - 1, 0, east), (0, 1, west))
        return [
            remote(
                source.at[held, :, lanes_of(tile, tile + 1)],
                target.at[s, held],
                side_send.at[turn, part, s],
                side_recv.at[turn, part, s],
                {"lon": to},
            )
            for tile, s, to in pairs
        ]

    def row_of(phase, row, i):
        return (again_ref if phase else mid_ref).at[row, :, run_lanes(phase, i)]

    def halo_copy(phase, d, i, r):
        row = r if d else rows - EDGE + r
        return remote(
            row_of(phase, row, i),
            halo_ref.at[phase, d, r, :, run_lanes(phase, i)],
            halo_send.at[phase, d, i, r],
            halo_recv.at[phase, d, i, r],
            {"lat": lat - 1 if d else lat + 1},
        )

    def pair_copy(phase, d, i):
        held = pl.ds(0 if d else rows - EDGE, EDGE)
        return remote(
            (again_ref if phase else mid_ref).at[held, :, run_lanes(phase, i)],
            halo_ref.at[phase, d, :, :, run_lanes(phase, i)],
            halo_send.at[phase, d, i, 0],
            halo_recv.at[phase, d, i, 0],
            {"lat": lat - 1 if d else lat + 1},
        )

    never = lat < 0
    sends_split = (is_low_mid, is_high_mid) if relayed else (never, never)
    takes_split = (is_high_mid, is_low_mid) if relayed else (never, never)

    def relay_copy(phase, d, i):
        row = 1 if d else rows - 1
        return remote(
            row_of(phase, row, i),
            relay_ref.at[phase, :, run_lanes(phase, i)],
            halo_send.at[phase, d, i, 1],
            relay_recv.at[phase, i],
            {"lat": relay_of},
        )

    def forward_copy(phase, i):
        return remote(
            relay_ref.at[phase, :, run_lanes(phase, i)],
            halo_ref.at[phase, relay_side, 1, :, run_lanes(phase, i)],
            relay_send.at[phase, i],
            halo_recv.at[phase, relay_side, i, 1],
            {"lat": relay_to},
        )

    def halo_start(phase, i):
        if relayed:

            @pl.when(is_low_mid)
            def _():
                relay_copy(phase, 0, i).start()

            @pl.when(is_high_mid)
            def _():
                relay_copy(phase, 1, i).start()

        for d in (1, 0):
            there = has_south if d else has_north

            @pl.when(jnp.logical_and(there, jnp.logical_not(sends_split[d])))
            def _():
                pair_copy(phase, d, i).start()

            @pl.when(sends_split[d])
            def _():
                halo_copy(phase, d, i, 0).start()

    def halo_sent(phase):
        for i in range(runs[phase]):
            for d in range(2):
                there = has_south if d else has_north

                @pl.when(jnp.logical_and(there, jnp.logical_not(sends_split[d])))
                def _():
                    pair_copy(phase, d, i).wait_send()

                @pl.when(sends_split[d])
                def _():
                    for r in range(EDGE):
                        halo_copy(phase, d, i, r).wait_send()

            if relayed:

                @pl.when(is_relay)
                def _():
                    forward_copy(phase, i).wait_send()

    def halo_arrive(phase, i):
        for d in range(2):

            @pl.when(jnp.logical_and(has[d], jnp.logical_not(takes_split[d])))
            def _():
                pair_copy(phase, d, i).wait_recv()

            @pl.when(takes_split[d])
            def _():
                for r in range(EDGE):
                    halo_copy(phase, d, i, r).wait_recv()

    def forward(phase, i):
        if relayed:
            relay_copy(phase, 0, i).wait_recv()
            forward_copy(phase, i).start()

    def forwards(phase, some):
        if relayed:

            @pl.when(is_relay)
            def _():
                for i in some:
                    forward(phase, i)

    def first_forwards(some):
        if relayed:

            @pl.when(is_relay)
            def _():
                for i in some:
                    forward(0, i)
                    if i + AHEAD < runs[0]:
                        halo_start(0, i + AHEAD)

    def spread(plane, target, scale=None):
        left = lax.broadcasted_iota(jnp.int32, (plane.shape[0], unit), 1) < unit // 2
        for j in range(tiles):
            a = jnp.broadcast_to(plane[:, 2 * j : 2 * j + 1], left.shape)
            b = jnp.broadcast_to(plane[:, 2 * j + 1 : 2 * j + 2], left.shape)
            v = jnp.where(left, a, b)
            if scale is not None:
                v = v * scale
            for r in range(plane.shape[0]):
                target(r, slice(j * unit, (j + 1) * unit), v[r : r + 1])

    def into(ref, offset=0):
        def put(r, at, v):
            ref[r + offset, :, at] = v

        return put

    def outer_faces():
        for n, ref in enumerate((lonc_ref, lonk_ref)):
            last = jnp.broadcast_to(comp_ref[1][:, n * cols : n * cols + 1], (rows, unit))
            for r in range(rows):
                ref[r, :, lanes:] = last[r : r + 1]

    def prepare_columns():
        mix = vertical_ref[...]
        gap = jnp.zeros((1, 1), jnp.float32)
        mix_ref[...] = jnp.concatenate([mix, gap, mix, gap], 1)
        light = jnp.concatenate([light_ref[...], light_ref[...]], 1)
        spread(day_ref[...].astype(jnp.float32), into(sun_ref), light)
        spread(raw_cnt_ref[...], into(cnt_ref))

    def prepare_rates():
        rates = jnp.concatenate([night_ref[...], photo_ref[...]], 0)
        top = rates.astype(jnp.bfloat16).astype(jnp.float32)
        w_ref[...] = jnp.concatenate([top, top, rates - top], 1).astype(jnp.bfloat16)
        shape = (species, species)
        same = lax.broadcasted_iota(jnp.int32, shape, 0) == lax.broadcasted_iota(jnp.int32, shape, 1)
        spread_loss = jnp.broadcast_to(raw_loss_ref[...], shape)
        loss_ref[...] = jnp.sum(jnp.where(same, spread_loss, 0.0), axis=1, keepdims=True)

    low = lax.broadcasted_iota(jnp.int32, (species, unit), 1) < unit // 2

    def swap(v):
        return pltpu.roll(v, unit // 2, 1)

    def lon_range(tile, store, e, first, last):
        before, here = tile(first - 1), tile(first)
        swapped = swap(here)
        behind = jnp.where(low, swap(before), swapped)
        flux, turned, cell = None, None, None
        for j in range(first, last + 1):
            if j < last:
                later = tile(j + 1)
                later_swapped = swap(later)
                ahead = jnp.where(low, swapped, later_swapped)
            else:
                later, later_swapped, ahead = here, swapped, swapped
            at = slice(j * unit, (j + 1) * unit)
            now = face_flux(lonc_ref[e, :, at], lonk_ref[e, :, at], before, behind, here, ahead)
            now_turned = swap(now)
            if j > first:
                upper = jnp.where(low, turned, now_turned)
                store(slice((j - 1) * unit, j * unit), cell - (upper - flux))
            flux, turned, cell = now, now_turned, here
            before, here, behind, swapped = here, later, ahead, later_swapped

    def lon_sweep(number, view, parts):
        def one(i, carry):
            tile, store, e = view(i)
            for first, last in parts:
                lon_range(tile, store, e, first, last)
            return carry

        lax.fori_loop(0, number, one, 0)

    whole = [(0, tiles)]
    middle, ends = [(1, tiles - 1)], [(0, 1), (tiles - 1, tiles)]

    def picker(inside, left, right):
        def tile(j):
            if j < 0:
                return left()
            if j == tiles:
                return right()
            return inside(j, slice(j * unit, (j + 1) * unit))

        return tile

    edge_rows = [r for first in (0, rows - EDGE) for r in range(first, first + EDGE)]

    def view(source, sides, target, inside):
        def at_row(i):
            row = i + EDGE if inside else i + (i // EDGE) * (rows - 2 * EDGE)
            tile = picker(
                lambda j, at: source[row, :, at],
                lambda: sides[0, row],
                lambda: sides[1, row],
            )

            def store(at, v):
                target[row, :, at] = v

            return tile, store, row

        return at_row

    raw_edge, raw_inner = (view(x_ref, side_raw, mid_ref, n) for n in (False, True))
    state_edge, state_inner = (view(state_ref, side_ref, again_ref, n) for n in (False, True))

    def lat_sweep(source, halo, store, spans, parts):
        def sweep(j):
            at = pl.ds(pl.multiple_of(j * unit, unit), unit)

            def cell(row):
                if row < 0:
                    return halo(0, row + EDGE, at)
                if row >= rows:
                    return halo(1, row - rows, at)
                return source[row, :, at]

            for first, last in spans:
                aa, a, b = cell(first - 2), cell(first - 1), cell(first)
                flux = None
                for row in range(first, last + 1):
                    bb = cell(row + 1)
                    now = face_flux(latc_ref[row, :, at], latk_ref[row, :, at], aa, a, b, bb)
                    if flux is not None:
                        store(row - 1, j, a - (now - flux))
                    flux = now
                    aa, a, b = a, b, bb

        count = sum(last - first for first, last in parts)
        each = count // len(parts)

        def one(t, carry):
            j = t + parts[0][0]
            if len(parts) > 1:
                j = j + (t // each) * (parts[1][0] - parts[0][0] - each)
            sweep(j)
            return carry

        lax.fori_loop(0, count, one, 0)

    edge_spans = ((0, EDGE), (rows - EDGE, rows))
    inner_spans = ((EDGE, rows - EDGE),)

    def first_halo(d, r, at):
        return halo_ref[0, d, r, :, at]

    def second_halo(d, r, at):
        return halo_ref[1, d, r, :, at]

    def into_state(row, j, v):
        state_ref[row, :, pl.ds(pl.multiple_of(j * unit, unit), unit)] = v

    def into_out(row, j, v):
        out_ref[row, :, pl.ds(pl.multiple_of(j * unit, unit), unit)] = v

    def chemistry(chunks):
        loss = loss_ref[...]

        def react(n, carry):
            for row, spans in chunks:
                for first, last in spans:
                    at = slice(first * unit, last * unit)
                    q = state_ref[row, :, at]
                    high = q.astype(jnp.bfloat16)
                    rest = (q - high.astype(jnp.float32)).astype(jnp.bfloat16)
                    both = jnp.dot(
                        w_ref[...],
                        jnp.concatenate([high, rest, high], 0),
                        preferred_element_type=jnp.float32,
                    )
                    top = q + both[:species] + sun_ref[row, :, at] * both[species:]
                    state_ref[row, :, at] = top / (1.0 + loss * q * q)
            return carry

        lax.fori_loop(0, CHEM, react, 0)
        for row, spans in chunks:
            places = [slice(t * unit, (t + 1) * unit) for span in spans for t in range(*span)]
            q = jnp.concatenate([state_ref[row, :, at] for at in places], 0)
            high = q.astype(jnp.bfloat16)
            rest = (q - high.astype(jnp.float32)).astype(jnp.bfloat16)
            terms = jnp.concatenate([high, rest, high], 1)
            mixed = [None for at in places]
            for n in range(0, KMAX, 2):
                both = jnp.dot(
                    terms,
                    power_ref[:, n * unit : (n + 2) * unit],
                    preferred_element_type=jnp.float32,
                )
                for t, at in enumerate(places):
                    held = slice(t * species, (t + 1) * species)
                    count = cnt_ref[row, :, at]
                    v = both[held, :unit]
                    if n > 0:
                        v = jnp.where(count > n, v, mixed[t])
                    mixed[t] = jnp.where(count > n + 1, both[held, unit:], v)
            for t, at in enumerate(places):
                state_ref[row, :, at] = mixed[t]

    def inner_chunks(row):
        return [(row, [(t, min(t + CHUNK, tiles))]) for t in range(0, tiles, CHUNK)]

    for n, ref in enumerate((lonc_ref, lonk_ref)):
        spread(comp_ref[0][:, n * cols : (n + 1) * cols], into(ref))
    lon_sweep(2 * EDGE, raw_edge, middle)
    for d in range(2):

        @pl.when(jnp.logical_not(has[d]))
        def _():
            for p in range(2):
                halo_ref[p, d] = jnp.zeros(halo_ref.shape[2:], jnp.float32)
            if d:
                comp_ref[2] = jnp.zeros(comp_ref.shape[1:], jnp.float32)

    peers = 2 + jnp.where(has_south, 1, 0) + jnp.where(has_north, 1, 0)
    if relayed:
        peers = peers + jnp.where(jnp.logical_or(is_mid, is_relay), 1, 0)
    pl.semaphore_wait(barrier, peers)

    comp_west.start()

    @pl.when(has_south)
    def _():
        comp_down.start()

    raw_sides = [side_copies(0, part) for part in range(3)]
    for pair in raw_sides:
        for copy in pair:
            copy.start()
    for i in range(2):
        halo_start(0, i)

    prepare_rates()
    prepare_columns()
    build_powers(unit, mix_ref, power_ref)
    for n, ref in enumerate((latc_ref, latk_ref)):
        spread(comp_ref[0][:, (n + 2) * cols : (n + 3) * cols], into(ref))
    comp_west.wait_recv()
    outer_faces()
    for pair in raw_sides[:2]:
        for copy in pair:
            copy.wait()
    lon_sweep(2 * EDGE, raw_edge, ends)
    for i in range(2, max(AHEAD, 2)):
        halo_start(0, i)
    others = True
    if relayed:
        others = jnp.logical_not(is_relay)

    @pl.when(others)
    def _():
        for i in range(max(AHEAD, 2), runs[0]):
            halo_start(0, i)

    first_forwards(range(2))
    for copy in raw_sides[2]:
        copy.wait()
    lon_sweep(inner, raw_inner, whole)

    @pl.when(has_north)
    def _():
        comp_down.wait_recv()

    for n, ref in enumerate((latc_ref, latk_ref)):
        spread(comp_ref[2][:1, (n + 2) * cols : (n + 3) * cols], into(ref, rows))
    lat_sweep(mid_ref, first_halo, into_state, inner_spans, whole)

    edge_sides = side_copies(1, 0) + side_copies(1, 1)
    ready, late, passed, done = 2, 0, 0, 0
    for k, parts in enumerate(swept):
        first_forwards(range(ready, min(ready + 2, runs[0])))
        ready += 2
        held = first_runs[2 * k : 2 * k + 2]
        for i in (2 * k, 2 * k + 1):
            halo_arrive(0, i)
        lat_sweep(mid_ref, first_halo, into_state, edge_spans, held)
        chunks = [(row, held) for row in edge_rows]
        beside = range(done, min(done + (BESIDE + (0,) * k)[k], inner))
        for i in beside:
            chunks += inner_chunks(i + EDGE)
        chemistry(chunks)
        if k == 1:
            for copy in edge_sides:
                copy.start()
        for i in beside:
            for copy in side_copies(1, i + 2, i + EDGE):
                copy.start()
        done += len(beside)
        if k == 2:
            for copy in edge_sides:
                copy.wait()
        forwards(1, range(late, passed))
        if parts:
            lon_sweep(2 * EDGE, state_edge, parts)
        number = sum(1 for run in second_runs if any(a <= run[0] < b for a, b in parts))
        for i in range(passed, passed + number):
            halo_start(1, i)
        late, passed = passed, passed + number

    for k in range(done, inner):
        chemistry(inner_chunks(k + EDGE))
        for copy in side_copies(1, k + 2, k + EDGE):
            copy.start()
    for k in range(inner):
        for copy in side_copies(1, k + 2, k + EDGE):
            copy.wait()
    lon_sweep(inner, state_inner, whole)
    forwards(1, range(late, runs[1]))
    lat_sweep(again_ref, second_halo, into_out, inner_spans, whole)
    for i in range(runs[1]):
        halo_arrive(1, i)
        lat_sweep(again_ref, second_halo, into_out, edge_spans, [second_runs[i]])

    comp_west.wait_send()

    @pl.when(has_south)
    def _():
        comp_down.wait_send()

    halo_sent(0)
    halo_sent(1)


def plan(tiles):
    pairs = tiles // 4
    order = [1, 0, *range(2, pairs)]
    first = [run for p in order for run in ((2 * p, 2 * p + 2), (tiles - 2 * p - 2, tiles - 2 * p))]
    swept = [[], [(1, 3), (tiles - 3, tiles - 1)]]
    for p in range(2, pairs):
        swept.append([(2 * p - 1, 2 * p + 1), (tiles - 2 * p - 1, tiles - 2 * p + 1)])
    swept[-1] = [(2 * pairs - 3, tiles - 2 * pairs + 3)]
    swept[2] = swept[2] + [(0, 1), (tiles - 1, tiles)]
    second = []
    for parts in swept:
        for a, b in parts:
            step = 3 if b - a > 4 else 2
            second += [(t, min(t + step, b)) for t in range(a, b, step)]
    return first, second, swept


def slopes(c, m):
    return jnp.where(c >= 0.0, 0.5 * (1.0 - c), -0.5 * (1.0 + c)) * m


def shards(
    tracers,
    courant,
    switches,
    day_flags,
    diffusion_counts,
    night_rates,
    photo_rates,
    level_light,
    self_loss,
    vertical_mixing,
):
    species, rows, lanes = tracers.shape
    levels = level_light.shape[0]
    cols = courant.shape[2]
    unit = 2 * levels
    tiles = lanes // unit
    runs = max(len(part) for part in plan(tiles)[:2])
    f32, i32, bf16 = jnp.float32, jnp.int32, jnp.bfloat16
    block = (rows, species, lanes)
    halo = (2, EDGE, species, lanes)
    dma = pltpu.SemaphoreType.DMA
    out = pl.pallas_call(
        functools.partial(kernel, unit),
        out_shape=jax.ShapeDtypeStruct(block, f32),
        in_specs=[pl.BlockSpec(memory_space=pltpu.VMEM)] * 10,
        out_specs=pl.BlockSpec(memory_space=pltpu.VMEM),
        scratch_shapes=[
            pltpu.VMEM((3, rows, 4 * cols), f32),
            pltpu.VMEM((rows, 1, lanes + unit), f32),
            pltpu.VMEM((rows, 1, lanes + unit), f32),
            pltpu.VMEM((rows + 1, 1, lanes), f32),
            pltpu.VMEM((rows + 1, 1, lanes), f32),
            pltpu.VMEM((rows, 1, lanes), f32),
            pltpu.VMEM((rows, 1, lanes), i32),
            pltpu.VMEM((1, unit), f32),
            pltpu.VMEM((2 * species, 3 * species), bf16),
            pltpu.VMEM((species, 1), f32),
            pltpu.VMEM(block, f32),
            pltpu.VMEM(block, f32),
            pltpu.VMEM(block, f32),
            pltpu.VMEM((2, rows, species, unit), f32),
            pltpu.VMEM((2, rows, species, unit), f32),
            pltpu.VMEM((2,) + halo, f32),
            pltpu.VMEM((2, species, lanes), f32),
            pltpu.VMEM((3 * unit, KMAX * unit), bf16),
            dma((3,)),
            dma((3,)),
            dma((2, rows, 2)),
            dma((2, rows, 2)),
            dma((2, 2, runs, EDGE)),
            dma((2, 2, runs, EDGE)),
            dma((2, runs)),
            dma((2, runs)),
        ],
        compiler_params=pltpu.CompilerParams(
            collective_id=0, has_side_effects=True, vmem_limit_bytes=48 * 1024 * 1024
        ),
    )(
        jnp.transpose(tracers, (1, 0, 2)),
        courant,
        switches,
        day_flags,
        diffusion_counts,
        night_rates,
        photo_rates,
        level_light[None],
        self_loss[None],
        vertical_mixing[None],
    )
    return jnp.transpose(out, (1, 0, 2))


def solution(mesh):
    grid = P(None, "lat", "lon")
    plane = P("lat", "lon")
    in_specs = (grid, grid, grid, plane, plane, P(), P(), P(), P(), P())
    return jax.shard_map(shards, mesh=mesh, in_specs=in_specs, out_specs=grid, check_vma=False)
```
